32 devices in a mesh: dp: 4 (over y, core), expert: 8 (over z, x).
Axes of the slice: x: 2, y: 2, z: 4, core: 2. Of those that a mesh axis runs over, the one named last changes fastest.
Arguments:
- tokens: bfloat16 [4096, 1024], P(('dp', 'expert')), may hold values from -6 to 6
- cotangent: bfloat16 [4096, 1024], P(('dp', 'expert')), may hold values from -2 to 2
- expert_ids: int32 [4096, 10], P(('dp', 'expert')), may hold values from 0 to 31, all different within a row; in each aligned block of 128 rows (0 to 127, 128 to 255, ...) at most 48 rows name the same one
- gate_weights: bfloat16 [4096, 10], P(('dp', 'expert')), may hold values from 0.019897461 to 0.29882812
- expert_weights: bfloat16 [32, 3, 1024, 512], P(('dp', 'expert')), may hold values from -0.1875 to 0.1875
- shared_weights: bfloat16 [3, 1024, 512], replicated, may hold values from -0.1875 to 0.1875
Outputs:
- grad_tokens: bfloat16 [4096, 1024], P(('dp', 'expert'))
- grad_gates: bfloat16 [4096, 10], P(('dp', 'expert'))
- grad_experts: bfloat16 [32, 3, 1024, 512], P(('dp', 'expert'))
- grad_shared: float32 [3, 1024, 512], P(None, 'dp')
The draws below stay inside these ranges and needn't reach their ends.
Inputs may be any that keep to these rules, and one draw needn't show every extreme that they name: `expert_ids`: each token names 10 different experts. Among the 128 tokens of one device no expert is named more than 48 times, and in some device's tokens some expert is named exactly 48 times.
All inputs are finite; a program needn't handle non-finite values.
Results may differ from the reference program's by a relative error of at most 0.0052.
Values may be sent and summed in bfloat16 or wider, within the bound.
No kernel may reach another device: no remote copies, remote signals or barrier semaphores. Data moves between devices by JAX's collectives and lax.ppermute only.
A program may use at most 128 MiB of HBM per device.

```python
import math
import jax
import jax.numpy as jnp
import numpy as np
from jax import lax

D = 1024
F = 512
F_SH = 512
TOP = 10
TOK_DEV = 128
TOKENS = 4096
EXPERTS = 32
CAP = 48
DEVICES = 32


def levels(own_key, extent, cuts, smallest, largest):
    level = 1.0
    for dim, shards_of in cuts:
        steps = jax.random.uniform(jax.random.fold_in(jax.random.fold_in(own_key, 6), dim), (shards_of,), jnp.float32, smallest / len(cuts), largest / len(cuts))
        level = level * jnp.repeat(jnp.exp(steps), extent[dim] // shards_of).reshape((-1,) + (1,) * (len(extent) - 1 - dim))
    return level


def deal_out(key, own, number, rows, number_of, top, reach, skew):
    order = jax.random.permutation(key, number_of)
    crowded, common = shares(number_of, rows * top, reach, skew, True), shares(number_of, rows * top, reach, skew, False)
    places = jnp.arange(number_of)

    def named(tallies, offset_by):
        used = int((tallies > 0).sum())
        fixed = max(1, used // 4)
        shifted = fixed + (places - fixed + offset_by * (used - fixed)) % max(1, number_of - fixed)
        return jnp.zeros((number_of,), jnp.int32).at[order[jnp.where(places < fixed, places, shifted)]].set(jnp.asarray(tallies, jnp.int32))

    tallies = jnp.where(number % 4 == 0, named(crowded, number // 4), named(common, number - number // 4 - 1))
    mixed = jax.random.permutation(jax.random.fold_in(own, 3), number_of)
    giver, sink = mixed[0:number_of // 2 * 2:2], mixed[1:number_of // 2 * 2:2]
    slack = jnp.minimum(tallies[giver] - 1, reach - tallies[sink]) // 2
    slack = jnp.where((giver == order[0]) | (sink == order[0]) | (tallies[sink] == 0), 0, jnp.maximum(slack, 0))
    shifted = jax.random.randint(jax.random.fold_in(own, 4), (number_of // 2,), 0, 1 << 20) % (slack + 1)
    tallies = tallies.at[giver].add(-shifted).at[sink].add(shifted)
    labels = jnp.searchsorted(jnp.cumsum(tallies), jnp.arange(rows * top), side="right").astype(jnp.int32)
    grid = labels.reshape(top, rows).T
    grid = grid[jax.random.permutation(jax.random.fold_in(own, 1), rows)]
    offset_by = jax.random.randint(jax.random.fold_in(own, 2), (rows, 1), 0, top)
    return jnp.take_along_axis(grid, (jnp.arange(top)[None, :] + offset_by) % top, axis=1)


def shares(amount, total, reach, skew, full):
    weights = [(1 << 20) // math.isqrt(standing ** skew) + 1 for standing in range(1, amount + 1)]
    largest = reach if full else min(reach, max(-(-total // amount), total * weights[0] // sum(weights)))
    least = 1 if total - largest >= amount - 1 else 0
    counts, surplus = [largest] + [least] * (amount - 1), total - largest - least * (amount - 1)
    while surplus > 0:
        candidates = [i for i in range(1, amount) if counts[i] < largest] or [i for i in range(1, amount) if counts[i] < reach]
        mass, budget = sum([weights[i] for i in candidates]), surplus
        for i in candidates:
            addition = min(reach - counts[i], max(1, budget * weights[i] // mass), surplus)
            counts[i] = counts[i] + addition
            surplus = surplus - addition
    return np.array(counts)


def bell_draw(own_key, extent, deviation, limit, cuts=(), kind=jnp.bfloat16):
    array = deviation * jax.random.normal(own_key, extent, jnp.float32)
    if cuts:
        array = array * levels(own_key, extent, cuts, -0.22, 0.18)
    return jnp.clip(array, -limit, limit).astype(kind)


def setup_inputs(seed: int = 0) -> dict:
    key_list = jax.random.split(jax.random.key(seed), 7)
    tokens = bell_draw(key_list[0], (TOKENS, D), 1.0, 6.0, ((0, 32),))
    cotangent = bell_draw(key_list[1], (TOKENS, D), 0.25, 2.0, ((0, 32),))
    expert_ids_keys = jax.random.split(jax.random.fold_in(key_list[2], 1), TOKENS // TOK_DEV)
    expert_ids_turns = jax.random.permutation(jax.random.fold_in(key_list[2], 3), TOKENS // TOK_DEV)
    expert_ids = jax.vmap(lambda own, number: deal_out(jax.random.fold_in(key_list[2], 2), own, number, TOK_DEV, EXPERTS, TOP, CAP, 2))(expert_ids_keys, expert_ids_turns).reshape((TOKENS, TOP))
    gate_weights = jnp.clip(jnp.exp(math.log(0.29882812) - 2.7092764 * jax.random.uniform(key_list[3], (TOKENS, TOP), jnp.float32) ** levels(key_list[3], (TOKENS, TOP), ((0, 32),), -0.2, 0.2)), 0.019897461, 0.29882812).astype(jnp.bfloat16)
    expert_weights = bell_draw(key_list[4], (EXPERTS, 3, D, F), D ** -0.5, 0.1875, ((0, 32),))
    shared_weights = bell_draw(key_list[5], (3, D, F_SH), D ** -0.5, 0.1875)
    return dict(tokens=tokens, cotangent=cotangent, expert_ids=expert_ids, gate_weights=gate_weights, expert_weights=expert_weights, shared_weights=shared_weights)


def silu_parts(pre):
    sigma = jax.nn.sigmoid(pre)
    return pre * sigma, sigma * (1.0 + pre * (1.0 - sigma))


def contract_rows(left, right):
    return jnp.dot(left.T, right, preferred_element_type=jnp.float32)


def expert_grads(inputs, upstream, scales, weight):
    hidden_units = weight.shape[2]
    paired = jnp.concatenate([weight[0], weight[1]], axis=1)
    gate_up = jnp.dot(inputs, paired, preferred_element_type=jnp.float32)
    pre_gate = gate_up[:, :hidden_units]
    pre_up = gate_up[:, hidden_units:]
    back = jnp.dot(upstream, weight[2], preferred_element_type=jnp.float32)
    activated, slope = silu_parts(pre_gate)
    hidden = activated * pre_up
    gate_grad = jnp.sum(hidden * back, axis=1)
    scaled = scales[:, None] * back
    grad_gate_in = (scaled * pre_up * slope).astype(jnp.bfloat16)
    grad_up_in = (scaled * activated).astype(jnp.bfloat16)
    both = jnp.concatenate([grad_gate_in, grad_up_in], axis=1)
    input_grad = jnp.dot(both, paired.T, preferred_element_type=jnp.float32)
    hidden_b = hidden.astype(jnp.bfloat16)
    scaled_up = (scales[:, None] * upstream.astype(jnp.float32)).astype(jnp.bfloat16)
    return input_grad, gate_grad, grad_gate_in, grad_up_in, hidden_b, scaled_up


def weight_terms(inputs, grad_gate_in, grad_up_in, scaled_up, hidden_b):
    return jnp.stack([contract_rows(inputs, grad_gate_in), contract_rows(inputs, grad_up_in),
                      contract_rows(scaled_up, hidden_b)], axis=0)


def reference(tokens, cotangent, expert_ids, gate_weights, expert_weights, shared_weights):
    pair_count = TOKENS * TOP
    row_ids = jnp.arange(TOKENS, dtype=jnp.int32)
    onehot = jnp.zeros((TOKENS, EXPERTS), jnp.int32).at[row_ids[:, None], expert_ids].add(1)
    blocked = onehot.reshape(TOKENS // TOK_DEV, TOK_DEV, EXPERTS)
    before = (jnp.cumsum(blocked, axis=1) - blocked).reshape(TOKENS, EXPERTS)
    slot_index = jnp.take_along_axis(before, expert_ids, axis=1).astype(jnp.int32)
    position = ((row_ids // TOK_DEV)[:, None] * CAP + slot_index).astype(jnp.int32)
    pair_index = jnp.arange(pair_count, dtype=jnp.int32).reshape(TOKENS, TOP)
    slot_table = jnp.full((EXPERTS, DEVICES * CAP), pair_count, jnp.int32).at[expert_ids, position].set(pair_index)
    padded_tokens = jnp.concatenate([tokens, jnp.zeros((1, D), jnp.bfloat16)], axis=0)
    padded_cotangent = jnp.concatenate([cotangent, jnp.zeros((1, D), jnp.bfloat16)], axis=0)
    padded_gates = jnp.concatenate([gate_weights.reshape(-1), jnp.zeros((1,), jnp.bfloat16)], axis=0)

    def visit(totals, packed):
        slot_rows, weight = packed
        token_rows = slot_rows // TOP
        inputs = padded_tokens[token_rows]
        parts = expert_grads(inputs, padded_cotangent[token_rows],
                             padded_gates[slot_rows].astype(jnp.float32), weight)
        w_grads = weight_terms(inputs, parts[2], parts[3], parts[5], parts[4]).astype(jnp.bfloat16)
        input_b = lax.optimization_barrier(parts[0].astype(jnp.bfloat16))
        gate_b = lax.optimization_barrier(parts[1].astype(jnp.bfloat16))
        input_total = totals[0].at[token_rows].add(input_b.astype(jnp.float32))
        gate_total = totals[1].at[slot_rows].set(gate_b.astype(jnp.float32))
        return (input_total, gate_total), w_grads

    init = (jnp.zeros((TOKENS + 1, D), jnp.float32), jnp.zeros((pair_count + 1,), jnp.float32))
    totals, grad_experts = lax.scan(visit, init, (slot_table, expert_weights))
    shared = expert_grads(tokens, cotangent, jnp.ones((TOKENS,), jnp.float32), shared_weights)
    grad_shared = weight_terms(tokens, shared[2], shared[3], shared[5], shared[4])
    grad_tokens = (totals[0][:TOKENS] + shared[0]).astype(jnp.bfloat16)
    grad_gates = totals[1][:pair_count].reshape(TOKENS, TOP).astype(jnp.bfloat16)
    return grad_tokens, grad_gates, grad_experts, grad_shared
```

```python
import functools

import jax
import jax.numpy as jnp
from jax import lax
from jax.experimental import pallas as pl
from jax.experimental.pallas import tpu as pltpu
from jax.sharding import PartitionSpec as P


def silu_parts(pre):
    sigma = jax.nn.sigmoid(pre)
    return (pre * sigma, sigma * (1.0 + pre * (1.0 - sigma)))


def contract_rows(left, right):
    return lax.dot_general(
        left, right, (((0,), (0,)), ((), ())), preferred_element_type=jnp.float32
    )


def expert_grads(inputs, upstream, scales, weight):
    hidden_units = weight.shape[2]
    paired = jnp.concatenate([weight[0], weight[1]], axis=1)
    gate_up = jnp.dot(inputs, paired, preferred_element_type=jnp.float32)
    pre_gate = gate_up[:, :hidden_units]
    pre_up = gate_up[:, hidden_units:]
    back = jnp.dot(upstream, weight[2], preferred_element_type=jnp.float32)
    activated, slope = silu_parts(pre_gate)
    hidden = activated * pre_up
    gate_grad = jnp.sum(hidden * back, axis=1)
    scaled = scales[:, None] * back
    grad_gate_in = (scaled * pre_up * slope).astype(jnp.bfloat16)
    grad_up_in = (scaled * activated).astype(jnp.bfloat16)
    both = jnp.concatenate([grad_gate_in, grad_up_in], axis=1)
    input_grad = lax.dot_general(
        both, paired, (((1,), (1,)), ((), ())), preferred_element_type=jnp.float32
    )
    hidden_b = hidden.astype(jnp.bfloat16)
    scaled_up = (scales[:, None] * upstream.astype(jnp.float32)).astype(jnp.bfloat16)
    return (input_grad, gate_grad, grad_gate_in, grad_up_in, hidden_b, scaled_up)


def weight_terms(inputs, grad_gate_in, grad_up_in, scaled_up, hidden_b):
    return jnp.stack(
        [
            contract_rows(inputs, grad_gate_in),
            contract_rows(inputs, grad_up_in),
            contract_rows(scaled_up, hidden_b),
        ],
        axis=0,
    )


def capacity_of(tok_rows, top_count, devices):
    return max(2, (6 * tok_rows * top_count + 5 * devices - 1) // (5 * devices))


def shards(tokens, cotangent, expert_ids, gate_weights, expert_weights, shared_weights):
    tok_rows, model_width = tokens.shape
    top_count = expert_ids.shape[1]
    data_count = lax.axis_size("dp")
    expert_count = lax.axis_size("expert")
    devices = data_count * expert_count
    capacity = capacity_of(tok_rows, top_count, devices)
    slot_total = devices * capacity
    pair_count = tok_rows * top_count
    row_ids = jnp.arange(tok_rows, dtype=jnp.int32)
    earlier_mask = (row_ids[:, None] > row_ids[None, :]).astype(jnp.bfloat16)
    padded_tokens = jnp.concatenate([tokens, jnp.zeros((1, model_width), jnp.bfloat16)], axis=0)
    padded_cotangent = jnp.concatenate(
        [cotangent, jnp.zeros((1, model_width), jnp.bfloat16)], axis=0
    )
    matches = expert_ids[:, :, None] == jnp.arange(devices, dtype=jnp.int32)
    per_token = jnp.sum(matches, axis=1).astype(jnp.bfloat16)
    before = jnp.dot(earlier_mask, per_token, preferred_element_type=jnp.float32)
    slot_index = jnp.sum(jnp.where(matches, before[:, None, :], 0.0), axis=2).astype(jnp.int32)
    position = expert_ids * capacity + slot_index
    slot_table = (
        jnp.full((slot_total,), pair_count, jnp.int32)
        .at[position.reshape(-1)]
        .set(jnp.arange(pair_count, dtype=jnp.int32))
    )
    token_index = slot_table // top_count
    padded_gates = jnp.concatenate(
        [gate_weights.reshape(-1), jnp.zeros((1,), jnp.bfloat16)], axis=0
    )
    send_tokens = padded_tokens[token_index].reshape(
        data_count, expert_count, capacity, model_width
    )
    send_cotangent = padded_cotangent[token_index].reshape(
        data_count, expert_count, capacity, model_width
    )
    send_gates = padded_gates[slot_table].reshape(data_count, expert_count, capacity)
    arrived = (
        lax.all_to_all(
            lax.all_to_all(send_tokens, "dp", split_axis=0, concat_axis=0, tiled=True),
            "expert",
            split_axis=1,
            concat_axis=1,
            tiled=True,
        ),
        lax.all_to_all(
            lax.all_to_all(send_cotangent, "dp", split_axis=0, concat_axis=0, tiled=True),
            "expert",
            split_axis=1,
            concat_axis=1,
            tiled=True,
        ),
        lax.all_to_all(
            lax.all_to_all(send_gates, "dp", split_axis=0, concat_axis=0, tiled=True),
            "expert",
            split_axis=1,
            concat_axis=1,
            tiled=True,
        ),
    )
    arrived_tokens = arrived[0].reshape(slot_total, model_width)
    routed = expert_grads(
        arrived_tokens,
        arrived[1].reshape(slot_total, model_width),
        arrived[2].reshape(slot_total).astype(jnp.float32),
        expert_weights[0],
    )
    grad_experts = weight_terms(arrived_tokens, routed[2], routed[3], routed[5], routed[4]).astype(
        jnp.bfloat16
    )[None]
    outgoing_input = (
        routed[0].astype(jnp.bfloat16).reshape(data_count, expert_count, capacity, model_width)
    )
    outgoing_gate = routed[1].astype(jnp.bfloat16).reshape(data_count, expert_count, capacity)
    returned = (
        lax.all_to_all(
            lax.all_to_all(outgoing_input, "dp", split_axis=0, concat_axis=0, tiled=True),
            "expert",
            split_axis=1,
            concat_axis=1,
            tiled=True,
        ),
        lax.all_to_all(
            lax.all_to_all(outgoing_gate, "dp", split_axis=0, concat_axis=0, tiled=True),
            "expert",
            split_axis=1,
            concat_axis=1,
            tiled=True,
        ),
    )
    flat_back = returned[0].reshape(slot_total, model_width)
    routed_sum = jnp.sum(flat_back[position].astype(jnp.float32), axis=1)
    grad_gates = returned[1].reshape(slot_total)[position]
    shared = expert_grads(tokens, cotangent, jnp.ones((tok_rows,), jnp.float32), shared_weights)
    grad_tokens = (routed_sum + shared[0]).astype(jnp.bfloat16)
    kept_rows = model_width // data_count
    shared_units = shared_weights.shape[2]
    upstream_cols = shared[5]
    kept = lax.psum_scatter(
        jnp.concatenate(
            [
                contract_rows(tokens, shared[2]),
                contract_rows(tokens, shared[3]),
                contract_rows(upstream_cols, shared[4]),
            ],
            axis=1,
        ),
        "dp",
        scatter_dimension=0,
        tiled=True,
    )
    totals = lax.psum(kept, "expert")
    grad_shared = jnp.transpose(totals.reshape(kept_rows, 3, shared_units), (1, 0, 2))
    return (grad_tokens, grad_gates, grad_experts, grad_shared)


def strict_upper(rows):
    r = lax.broadcasted_iota(jnp.int32, (rows, rows), 0)
    c = lax.broadcasted_iota(jnp.int32, (rows, rows), 1)
    return (r < c).astype(jnp.bfloat16)


def dot32(left, right, dims=((1,), (0,))):
    return lax.dot_general(left, right, (dims, ((), ())), preferred_element_type=jnp.float32)


def route_kernel(n, cap, gates, *refs):
    pieces, (w_own, w_sib) = refs[:n], refs[n : n + 2]
    parts, (gate_out, xs, sy, gg, gu, hb) = refs[n + 2 : 2 * n + 2], refs[2 * n + 2 : 2 * n + 8]
    onehot, yslot, gslot, ig = refs[2 * n + 8 :]
    rows = gates.shape[2]
    named = jnp.where(gates[...] > 0, 1.0, 0.0)
    before = dot32(named.reshape(2 * n, rows).astype(jnp.bfloat16), strict_upper(rows))
    before = before.reshape(n, 2, rows)
    slot = lax.broadcasted_iota(jnp.int32, (cap, rows), 0).astype(jnp.float32)
    for p in range(n):
        for j in range(2):
            hit = (before[p, j][None, :] == slot) & (named[p, j][None, :] > 0)
            hit = jnp.where(hit, 1.0, 0.0)
            onehot[p, j * cap : (j + 1) * cap] = hit.astype(jnp.bfloat16)
            gslot[j, p * cap : (p + 1) * cap] = jnp.sum(
                hit * gates[p, j].astype(jnp.float32)[None, :], axis=1, keepdims=True
            )
        picked_x = dot32(onehot[p], pieces[p][0]).astype(jnp.bfloat16)
        picked_y = dot32(onehot[p], pieces[p][1])
        for j in range(2):
            here = slice(p * cap, (p + 1) * cap)
            there = slice(j * cap, (j + 1) * cap)
            xs[j, here] = picked_x[there]
            yslot[j, here] = picked_y[there].astype(jnp.bfloat16)
            sy[j, here] = (picked_y[there] * gslot[j, here]).astype(jnp.bfloat16)
    hidden_units = w_own.shape[2]
    tile = min(256, hidden_units)
    for j, w in enumerate((w_own, w_sib)):
        gate_grad = jnp.zeros((n * cap, 1), jnp.float32)
        for f in range(0, hidden_units, tile):
            cols = slice(f, f + tile)
            pre_gate = dot32(xs[j], w[0, :, cols])
            pre_up = dot32(xs[j], w[1, :, cols])
            back = dot32(yslot[j], w[2, :, cols])
            activated, slope = silu_parts(pre_gate)
            hidden = activated * pre_up
            gate_grad += jnp.sum(hidden * back, axis=1, keepdims=True)
            scaled = gslot[j] * back
            gg[j, :, cols] = (scaled * pre_up * slope).astype(jnp.bfloat16)
            gu[j, :, cols] = (scaled * activated).astype(jnp.bfloat16)
            hb[j, :, cols] = hidden.astype(jnp.bfloat16)
        ig[j] = (
            dot32(gg[j], w[0], ((1,), (1,))) + dot32(gu[j], w[1], ((1,), (1,)))
        ).astype(jnp.bfloat16)
        for p in range(n):
            hit = onehot[p, j * cap : (j + 1) * cap].astype(jnp.float32)
            gate_out[p, j : j + 1] = jnp.sum(
                hit * gate_grad[p * cap : (p + 1) * cap], axis=0, keepdims=True
            )
    for p in range(n):
        both = jnp.concatenate([ig[j, p * cap : (p + 1) * cap] for j in range(2)], axis=0)
        parts[p][...] = dot32(onehot[p], both, ((0,), (0,))).astype(parts[p].dtype)


def route(cap, gates, pieces, w_own, w_sib):
    n, rows, width = len(pieces), pieces[0].shape[1], pieces[0].shape[2]
    hidden_units = w_own.shape[2]
    slots = n * cap
    shape = jax.ShapeDtypeStruct
    bf = jnp.bfloat16
    out_shape = [shape((rows, width), jnp.float32)] + [shape((rows, width), bf)] * (n - 1)
    out_shape += [shape((n, 2, rows), jnp.float32)]
    out_shape += [shape((2, slots, width), bf)] * 2 + [shape((2, slots, hidden_units), bf)] * 3
    flops = 2 * 2 * slots * width * hidden_units * 5
    outs = pl.pallas_call(
        functools.partial(route_kernel, n, cap),
        out_shape=out_shape,
        scratch_shapes=[
            pltpu.VMEM((n, 2 * cap, rows), bf),
            pltpu.VMEM((2, slots, width), bf),
            pltpu.VMEM((2, slots, 1), jnp.float32),
            pltpu.VMEM((2, slots, width), bf),
        ],
        cost_estimate=pl.CostEstimate(
            flops=flops, bytes_accessed=4 * w_own.size + 2 * slots * width * 8, transcendentals=0
        ),
        name="route",
    )(gates, *pieces, w_own, w_sib)
    return outs[:n], outs[n], outs[n + 1 :]


def common_kernel(n, first, last, where_ref, *refs):
    pieces, w, refs = refs[:n], refs[n], refs[n + 1 :]
    if not first:
        total_in, refs = refs[0], refs[1:]
    if first:
        own_grad, refs = refs[0], refs[1:]
    if last:
        (mine, other), refs = refs[:2], refs[2:]
    else:
        total, refs = refs[0], refs[1:]
    x, y, gg, gu, hb = refs
    rows = pieces[0].shape[1]
    for p in range(n):
        x[p * rows : (p + 1) * rows] = pieces[p][0]
        y[p * rows : (p + 1) * rows] = pieces[p][1]
    hidden_units = w.shape[2]
    tile = min(256, hidden_units)
    for f in range(0, hidden_units, tile):
        cols = slice(f, f + tile)
        pre_gate = dot32(x[...], w[0, :, cols])
        pre_up = dot32(x[...], w[1, :, cols])
        back = dot32(y[...], w[2, :, cols])
        activated, slope = silu_parts(pre_gate)
        gg[:, cols] = (back * pre_up * slope).astype(jnp.bfloat16)
        gu[:, cols] = (back * activated).astype(jnp.bfloat16)
        hb[:, cols] = (activated * pre_up).astype(jnp.bfloat16)
    if first:
        own_grad[...] = dot32(gg[:rows], w[0], ((1,), (1,))) + dot32(gu[:rows], w[1], ((1,), (1,)))
    kept = total_in.shape[1] if not first else total.shape[1]
    keep = pl.ds(pl.multiple_of(where_ref[0] * kept, kept), kept)
    xk, yk = x[:, keep], y[:, keep]
    for i, (left, right) in enumerate(((xk, gg), (xk, gu), (yk, hb))):
        term = dot32(left, right[...], ((0,), (0,)))
        if not first:
            term = term + total_in[i]
        if last:
            half = kept // 2

            @pl.when(where_ref[1] == 0)
            def _():
                mine[i] = term[:half]
                other[i] = term[half:]

            @pl.when(where_ref[1] == 1)
            def _():
                mine[i] = term[half:]
                other[i] = term[:half]
        else:
            total[i] = term


def common(where_at, kept, pieces, w, total, last):
    first = total is None
    n, rows, width = len(pieces), pieces[0].shape[1], pieces[0].shape[2]
    hidden_units = w.shape[2]
    shape = jax.ShapeDtypeStruct
    out_shape = [shape((rows, width), jnp.float32)] if first else []
    if last:
        out_shape += [shape((3, kept // 2, hidden_units), jnp.float32)] * 2
    else:
        out_shape += [shape((3, kept, hidden_units), jnp.float32)]
    args = list(pieces) + [w] + ([] if first else [total])
    flops = 2 * n * rows * hidden_units * 3 * (width + kept)
    return pl.pallas_call(
        functools.partial(common_kernel, n, first, last),
        out_shape=out_shape,
        in_specs=[pl.BlockSpec(memory_space=pltpu.SMEM)]
        + [pl.BlockSpec(memory_space=pltpu.VMEM)] * len(args),
        scratch_shapes=[pltpu.VMEM((n * rows, width), jnp.bfloat16)] * 2
        + [pltpu.VMEM((n * rows, hidden_units), jnp.bfloat16)] * 3,
        cost_estimate=pl.CostEstimate(
            flops=flops, bytes_accessed=2 * w.size + n * rows * width * 4, transcendentals=0
        ),
        name="common",
    )(where_at, *args)


def weights_kernel(groups, j, received, *refs):
    saved, refs = refs[: 5 * groups], refs[5 * groups :]
    came, out = (refs[0], refs[1]) if received else (None, refs[0])
    for i, (left, right) in enumerate(((0, 2), (0, 3), (1, 4))):
        total = None
        for g in range(groups):
            term = dot32(saved[5 * g + left][j], saved[5 * g + right][j], ((0,), (0,)))
            total = term if total is None else total + term
        if received:
            total = total + came[i].astype(jnp.float32)
        out[i] = total.astype(jnp.bfloat16)


def weights(saved, j, came):
    groups = len(saved)
    flat = [a for group in saved for a in group]
    width, hidden_units = flat[0].shape[2], flat[2].shape[2]
    slots = sum(group[0].shape[1] for group in saved)
    args = flat + ([came] if came is not None else [])
    return pl.pallas_call(
        functools.partial(weights_kernel, groups, j, came is not None),
        out_shape=jax.ShapeDtypeStruct((3, width, hidden_units), jnp.bfloat16),
        in_specs=[pl.BlockSpec((1,) + a.shape[1:], lambda j=j: (j, 0, 0)) for a in flat]
        if False
        else [pl.BlockSpec(memory_space=pltpu.VMEM)] * len(args),
        cost_estimate=pl.CostEstimate(
            flops=6 * slots * width * hidden_units,
            bytes_accessed=slots * (4 * width + 6 * hidden_units),
            transcendentals=0,
        ),
        name="weights",
    )(*args)


def shared_rows(tokens, cotangent, expert_ids, gate_weights, expert_weights, shared_weights):
    rows, width = tokens.shape
    top_count = expert_ids.shape[1]
    data_count, expert_count = lax.axis_size("dp"), lax.axis_size("expert")
    devices = data_count * expert_count
    cap = capacity_of(rows, top_count, devices)
    planes = expert_count // 2
    bf, f32 = jnp.bfloat16, jnp.float32
    me_dp, me_ex = lax.axis_index("dp"), lax.axis_index("expert")
    across_x = [(e, e ^ 1) for e in range(expert_count)]
    around_z = [(e, (e + 2) % expert_count) for e in range(expert_count)]
    across_y = [(d, d ^ 2) for d in range(data_count)]
    across_core = [(d, d ^ 1) for d in range(data_count)]
    px = lambda a: lax.ppermute(a, "expert", across_x)
    pz = lambda a: lax.ppermute(a, "expert", around_z)
    py = lambda a: lax.ppermute(a, "dp", across_y)
    pc = lambda a: lax.ppermute(a, "dp", across_core)

    w_own = expert_weights[0]
    own = jnp.stack([tokens, cotangent])
    w_sib = pc(w_own)

    matches = expert_ids[:, :, None] == jnp.arange(devices, dtype=jnp.int32)
    by_expert = jnp.sum(jnp.where(matches, gate_weights[:, :, None].astype(f32), 0.0), axis=1)
    by_expert = by_expert.T.astype(bf).reshape(data_count // 2, 2, expert_count, rows)
    outward = jnp.stack([by_expert, by_expert[:, ::-1]], axis=3).reshape(devices, 2, rows)
    inward = lax.all_to_all(outward, ("dp", "expert"), 0, 0, tiled=True)
    order = []
    for s in range(planes):
        plane = (me_ex // 2 + planes - s) % planes
        for dy, dx in ((0, 0), (0, 1), (1, 0), (1, 1)):
            source = (me_dp ^ (2 * dy)) * expert_count + plane * 2 + (me_ex % 2 ^ dx)
            order.append(source)
    pick = jnp.stack(order)[:, None] == jnp.arange(devices, dtype=jnp.int32)[None, :]
    pick = pick.astype(bf)
    gates = jnp.dot(pick, inward.reshape(devices, 2 * rows), preferred_element_type=f32)
    gates = gates.reshape(planes, 4, 2, rows)

    col, xs, ys, ds = [own], [], [], []
    for s in range(planes):
        if s:
            col.append(pz(col[s - 1]))
        xs.append(px(col[s]))
        ys.append(py(col[s]))
        if s < max(1, planes // 2):
            ds.append(jnp.stack([px(ys[s][0]), py(xs[s][1])]))
        else:
            ds.append(pz(ds[s - 1]))

    where_at = jnp.stack([me_dp // 2, me_dp % 2]).astype(jnp.int32)
    kept = 2 * (width // data_count)
    total, shared_grad, saved, gate_grads = None, None, [], []
    carry, carry_d, final = None, None, None
    half = width // 2
    for s in range(planes):
        pieces = (col[s], xs[s], ys[s], ds[s])
        (c, x, y, d), gate_grad, keep = route(cap, gates[s], pieces, w_own, w_sib)
        saved.append(keep)
        gate_grads.append(gate_grad)
        outs = common(where_at, kept, pieces, shared_weights, total, s == planes - 1)
        if s == 0:
            shared_grad, total = outs
        elif s < planes - 1:
            total = outs[0]
        else:
            mine, other = outs
        if carry_d is not None:
            d = (d.astype(f32) + carry_d.astype(f32)).astype(bf)
        if 0 < s < planes - 1:
            carry_d = pz(d)
        else:
            from_x, from_y = px(d[:, :half]), py(d[:, half:])
            y = jnp.concatenate([(y[:, :half].astype(f32) + from_x.astype(f32)).astype(bf), y[:, half:]], axis=1)
            x = jnp.concatenate([x[:, :half], (x[:, half:].astype(f32) + from_y.astype(f32)).astype(bf)], axis=1)
        c = c + px(x).astype(f32) + py(y).astype(f32)
        if s == 0:
            final = c
        else:
            if carry is not None:
                c = c + carry.astype(f32)
            carry = pz(c.astype(bf))
    if carry is not None:
        final = final + carry.astype(f32)
    grad_tokens = (final + shared_grad).astype(bf)

    grad_shared = mine + pc(other)
    came = pc(weights(saved, 1, None))
    grad_experts = weights(saved, 0, came)[None]

    back = jnp.stack(gate_grads).reshape(4 * planes, 2 * rows).astype(bf)
    back = lax.dot_general(pick, back, (((0,), (0,)), ((), ())), preferred_element_type=f32)
    back = lax.all_to_all(back.astype(bf).reshape(devices, 2, rows), ("dp", "expert"), 0, 0, tiled=True)
    back = back.astype(f32).reshape(data_count // 2, 2, expert_count, 2, rows)
    by_expert = back[:, :, :, 0] + back[:, ::-1, :, 1]
    by_expert = by_expert.reshape(devices, rows).T
    grad_gates = jnp.sum(jnp.where(matches, by_expert[:, None, :], 0.0), axis=2).astype(bf)
    return (grad_tokens, grad_gates, grad_experts, grad_shared)


def solution(mesh):
    placed = (
        P(("dp", "expert"), None),
        P(("dp", "expert"), None),
        P(("dp", "expert"), None),
        P(("dp", "expert"), None),
        P(("dp", "expert"), None, None, None),
        P(),
    )
    data_count, expert_count = mesh.shape["dp"], mesh.shape["expert"]

    def body(tokens, cotangent, expert_ids, gate_weights, expert_weights, shared_weights):
        rows = tokens.shape[0] * data_count * expert_count
        slots = data_count * expert_count * capacity_of(
            tokens.shape[0], expert_ids.shape[1], data_count * expert_count
        )
        share = data_count == 4 and expert_count % 4 == 0 and rows <= 4 * slots
        plan = shared_rows if share else shards
        return plan(tokens, cotangent, expert_ids, gate_weights, expert_weights, shared_weights)

    return jax.shard_map(
        body,
        mesh=mesh,
        in_specs=placed,
        out_specs=(
            P(("dp", "expert"), None),
            P(("dp", "expert"), None),
            P(("dp", "expert"), None, None, None),
            P(None, "dp", None),
        ),
        check_vma=False,
    )
```

```python
import functools

import jax
import jax.numpy as jnp
from jax import lax
from jax.experimental import pallas as pl
from jax.experimental.pallas import tpu as pltpu
from jax.sharding import PartitionSpec as P


def silu_parts(pre):
    sigma = jax.nn.sigmoid(pre)
    return (pre * sigma, sigma * (1.0 + pre * (1.0 - sigma)))


def contract_rows(left, right):
    return lax.dot_general(
        left, right, (((0,), (0,)), ((), ())), preferred_element_type=jnp.float32
    )


def expert_grads(inputs, upstream, scales, weight):
    hidden_units = weight.shape[2]
    paired = jnp.concatenate([weight[0], weight[1]], axis=1)
    gate_up = jnp.dot(inputs, paired, preferred_element_type=jnp.float32)
    pre_gate = gate_up[:, :hidden_units]
    pre_up = gate_up[:, hidden_units:]
    back = jnp.dot(upstream, weight[2], preferred_element_type=jnp.float32)
    activated, slope = silu_parts(pre_gate)
    hidden = activated * pre_up
    gate_grad = jnp.sum(hidden * back, axis=1)
    scaled = scales[:, None] * back
    grad_gate_in = (scaled * pre_up * slope).astype(jnp.bfloat16)
    grad_up_in = (scaled * activated).astype(jnp.bfloat16)
    both = jnp.concatenate([grad_gate_in, grad_up_in], axis=1)
    input_grad = lax.dot_general(
        both, paired, (((1,), (1,)), ((), ())), preferred_element_type=jnp.float32
    )
    hidden_b = hidden.astype(jnp.bfloat16)
    scaled_up = (scales[:, None] * upstream.astype(jnp.float32)).astype(jnp.bfloat16)
    return (input_grad, gate_grad, grad_gate_in, grad_up_in, hidden_b, scaled_up)


def weight_terms(inputs, grad_gate_in, grad_up_in, scaled_up, hidden_b):
    return jnp.stack(
        [
            contract_rows(inputs, grad_gate_in),
            contract_rows(inputs, grad_up_in),
            contract_rows(scaled_up, hidden_b),
        ],
        axis=0,
    )


def capacity_of(tok_rows, top_count, devices):
    return max(2, (6 * tok_rows * top_count + 5 * devices - 1) // (5 * devices))


def shards(tokens, cotangent, expert_ids, gate_weights, expert_weights, shared_weights):
    tok_rows, model_width = tokens.shape
    top_count = expert_ids.shape[1]
    data_count = lax.axis_size("dp")
    expert_count = lax.axis_size("expert")
    devices = data_count * expert_count
    capacity = capacity_of(tok_rows, top_count, devices)
    slot_total = devices * capacity
    pair_count = tok_rows * top_count
    row_ids = jnp.arange(tok_rows, dtype=jnp.int32)
    earlier_mask = (row_ids[:, None] > row_ids[None, :]).astype(jnp.bfloat16)
    padded_tokens = jnp.concatenate([tokens, jnp.zeros((1, model_width), jnp.bfloat16)], axis=0)
    padded_cotangent = jnp.concatenate(
        [cotangent, jnp.zeros((1, model_width), jnp.bfloat16)], axis=0
    )
    matches = expert_ids[:, :, None] == jnp.arange(devices, dtype=jnp.int32)
    per_token = jnp.sum(matches, axis=1).astype(jnp.bfloat16)
    before = jnp.dot(earlier_mask, per_token, preferred_element_type=jnp.float32)
    slot_index = jnp.sum(jnp.where(matches, before[:, None, :], 0.0), axis=2).astype(jnp.int32)
    position = expert_ids * capacity + slot_index
    slot_table = (
        jnp.full((slot_total,), pair_count, jnp.int32)
        .at[position.reshape(-1)]
        .set(jnp.arange(pair_count, dtype=jnp.int32))
    )
    token_index = slot_table // top_count
    padded_gates = jnp.concatenate(
        [gate_weights.reshape(-1), jnp.zeros((1,), jnp.bfloat16)], axis=0
    )
    send_tokens = padded_tokens[token_index].reshape(
        data_count, expert_count, capacity, model_width
    )
    send_cotangent = padded_cotangent[token_index].reshape(
        data_count, expert_count, capacity, model_width
    )
    send_gates = padded_gates[slot_table].reshape(data_count, expert_count, capacity)
    arrived = (
        lax.all_to_all(
            lax.all_to_all(send_tokens, "dp", split_axis=0, concat_axis=0, tiled=True),
            "expert",
            split_axis=1,
            concat_axis=1,
            tiled=True,
        ),
        lax.all_to_all(
            lax.all_to_all(send_cotangent, "dp", split_axis=0, concat_axis=0, tiled=True),
            "expert",
            split_axis=1,
            concat_axis=1,
            tiled=True,
        ),
        lax.all_to_all(
            lax.all_to_all(send_gates, "dp", split_axis=0, concat_axis=0, tiled=True),
            "expert",
            split_axis=1,
            concat_axis=1,
            tiled=True,
        ),
    )
    arrived_tokens = arrived[0].reshape(slot_total, model_width)
    routed = expert_grads(
        arrived_tokens,
        arrived[1].reshape(slot_total, model_width),
        arrived[2].reshape(slot_total).astype(jnp.float32),
        expert_weights[0],
    )
    grad_experts = weight_terms(arrived_tokens, routed[2], routed[3], routed[5], routed[4]).astype(
        jnp.bfloat16
    )[None]
    outgoing_input = (
        routed[0].astype(jnp.bfloat16).reshape(data_count, expert_count, capacity, model_width)
    )
    outgoing_gate = routed[1].astype(jnp.bfloat16).reshape(data_count, expert_count, capacity)
    returned = (
        lax.all_to_all(
            lax.all_to_all(outgoing_input, "dp", split_axis=0, concat_axis=0, tiled=True),
            "expert",
            split_axis=1,
            concat_axis=1,
            tiled=True,
        ),
        lax.all_to_all(
            lax.all_to_all(outgoing_gate, "dp", split_axis=0, concat_axis=0, tiled=True),
            "expert",
            split_axis=1,
            concat_axis=1,
            tiled=True,
        ),
    )
    flat_back = returned[0].reshape(slot_total, model_width)
    routed_sum = jnp.sum(flat_back[position].astype(jnp.float32), axis=1)
    grad_gates = returned[1].reshape(slot_total)[position]
    shared = expert_grads(tokens, cotangent, jnp.ones((tok_rows,), jnp.float32), shared_weights)
    grad_tokens = (routed_sum + shared[0]).astype(jnp.bfloat16)
    kept_rows = model_width // data_count
    shared_units = shared_weights.shape[2]
    upstream_cols = shared[5]
    kept = lax.psum_scatter(
        jnp.concatenate(
            [
                contract_rows(tokens, shared[2]),
                contract_rows(tokens, shared[3]),
                contract_rows(upstream_cols, shared[4]),
            ],
            axis=1,
        ),
        "dp",
        scatter_dimension=0,
        tiled=True,
    )
    totals = lax.psum(kept, "expert")
    grad_shared = jnp.transpose(totals.reshape(kept_rows, 3, shared_units), (1, 0, 2))
    return (grad_tokens, grad_gates, grad_experts, grad_shared)


def strict_upper(rows):
    r = lax.broadcasted_iota(jnp.int32, (rows, rows), 0)
    c = lax.broadcasted_iota(jnp.int32, (rows, rows), 1)
    return (r < c).astype(jnp.bfloat16)


def dot32(left, right, dims=((1,), (0,))):
    return lax.dot_general(left, right, (dims, ((), ())), preferred_element_type=jnp.float32)


def route_kernel(s, n, cap, at_ref, gates_ref, *refs):
    pieces, w_refs = refs[:n], refs[n : n + 2]
    parts = refs[n + 2 : 2 * n + 2]
    xs, sy, gg, gu, hb, onehot, yslot, ig = refs[2 * n + 2 :]
    rows, width = gates_ref.shape[3], pieces[0].shape[1]
    gates = gates_ref[s]
    named = jnp.where(gates > 0, 1.0, 0.0)
    before = dot32(named.reshape(2 * n, rows).astype(jnp.bfloat16), strict_upper(rows))
    before = before.reshape(n, 2, rows)
    slot = lax.broadcasted_iota(jnp.int32, (cap, rows), 0).astype(jnp.float32)
    scales = [[], []]
    for p in range(n):
        for j in range(2):
            hit = (before[p, j][None, :] == slot) & (named[p, j][None, :] > 0)
            hit = jnp.where(hit, 1.0, 0.0)
            onehot[p, j * cap : (j + 1) * cap] = hit.astype(jnp.bfloat16)
            scales[j].append(jnp.sum(hit * gates[p, j][None, :], axis=1, keepdims=True))
        picked_x = dot32(onehot[p], pieces[p][:rows]).astype(jnp.bfloat16)
        picked_y = dot32(onehot[p], pieces[p][rows:])
        for j in range(2):
            here = slice(p * cap, (p + 1) * cap)
            there = slice(j * cap, (j + 1) * cap)
            xs[j, here] = picked_x[there]
            yslot[j, here] = picked_y[there].astype(jnp.bfloat16)
            sy[j, here] = (picked_y[there] * scales[j][p]).astype(jnp.bfloat16)
    hidden_units = w_refs[0].shape[2]
    tile = min(256, hidden_units)
    grads = []
    for j, w in enumerate(w_refs):
        scale = jnp.concatenate(scales[j], axis=0)
        gate_grad = jnp.zeros((n * cap, 1), jnp.float32)
        for f in range(0, hidden_units, tile):
            cols = slice(f, f + tile)
            pre_gate = dot32(xs[j], w[0, :, cols])
            pre_up = dot32(xs[j], w[1, :, cols])
            back = dot32(yslot[j], w[2, :, cols])
            activated, slope = silu_parts(pre_gate)
            hidden = activated * pre_up
            gate_grad += jnp.sum(hidden * back, axis=1, keepdims=True)
            scaled = scale * back
            gg[j, :, cols] = (scaled * pre_up * slope).astype(jnp.bfloat16)
            gu[j, :, cols] = (scaled * activated).astype(jnp.bfloat16)
            hb[j, :, cols] = hidden.astype(jnp.bfloat16)
        ig[j] = (
            dot32(gg[j], w[0], ((1,), (1,))) + dot32(gu[j], w[1], ((1,), (1,)))
        ).astype(jnp.bfloat16)
        grads.append(gate_grad)
    extra = parts[0].shape[0] - rows
    row = lax.broadcasted_iota(jnp.int32, (extra, width), 0)
    block = lax.broadcasted_iota(jnp.int32, (extra, width), 1) // rows
    for p in range(n):
        tail = jnp.zeros((extra, width), jnp.float32)
        for j in range(2):
            here = slice(p * cap, (p + 1) * cap)
            hit = onehot[p, j * cap : (j + 1) * cap].astype(jnp.float32)
            line = jnp.sum(hit * grads[j][here], axis=0, keepdims=True)
            line = jnp.concatenate([line] * (width // rows), axis=1)
            mine = (row == at_ref[2 * j]) & (block == at_ref[2 * j + 1])
            tail = tail + jnp.where(mine, line, 0.0)
        both = jnp.concatenate([ig[j, here] for j in range(2)], axis=0)
        parts[p][:rows] = dot32(onehot[p], both, ((0,), (0,))).astype(parts[p].dtype)
        parts[p][rows:] = tail.astype(jnp.bfloat16).astype(parts[p].dtype)


MIB = 1024 * 1024
IN_SMEM = pl.BlockSpec(memory_space=pltpu.SMEM)
IN_VMEM = pl.BlockSpec(memory_space=pltpu.VMEM)


def route(s, cap, extra, at, gates, pieces, w_own, w_sib):
    n, rows, width = len(pieces), gates.shape[3], pieces[0].shape[1]
    hidden_units = w_own.shape[2]
    slots = n * cap
    shape, scratch = jax.ShapeDtypeStruct, pltpu.VMEM
    bf = jnp.bfloat16
    out_shape = [shape((rows + extra, width), jnp.float32)]
    out_shape += [shape((rows + extra, width), bf)] * (n - 1)
    out_shape += [shape((2, slots, width), bf)] * 2 + [shape((2, slots, hidden_units), bf)] * 3
    outs = pl.pallas_call(
        functools.partial(route_kernel, s, n, cap),
        out_shape=out_shape,
        in_specs=[IN_SMEM] + [IN_VMEM] * (n + 3),
        out_specs=[IN_VMEM] * (n + 5),
        scratch_shapes=[
            scratch((n, 2 * cap, rows), bf),
            scratch((2, slots, width), bf),
            scratch((2, slots, width), bf),
        ],
        cost_estimate=pl.CostEstimate(
            flops=20 * slots * width * hidden_units,
            bytes_accessed=4 * w_own.size + 16 * slots * width,
            transcendentals=0,
        ),
        compiler_params=pltpu.CompilerParams(vmem_limit_bytes=20 * MIB),
        name="route",
    )(at, gates, *pieces, w_own, w_sib)
    return outs[:n], outs[n:]


def common_kernel(n, first, last, where_ref, *refs):
    pieces, w, refs = refs[:n], refs[n], refs[n + 1 :]
    (own_grad,), refs = (refs[:1], refs[1:]) if first else ((None,), refs)
    (total_in,), refs = ((None,), refs) if first else (refs[:1], refs[1:])
    outs, (x, y, gg, gu, hb) = refs[:-5], refs[-5:]
    rows = pieces[0].shape[0] // 2
    for p in range(n):
        x[p * rows : (p + 1) * rows] = pieces[p][:rows]
        y[p * rows : (p + 1) * rows] = pieces[p][rows:]
    hidden_units = w.shape[2]
    tile = min(256, hidden_units)
    chunk = 4 * rows
    for r in range(0, n * rows, chunk):
        at = slice(r, r + chunk)
        for f in range(0, hidden_units, tile):
            cols = slice(f, f + tile)
            pre_gate = dot32(x[at], w[0, :, cols])
            pre_up = dot32(x[at], w[1, :, cols])
            back = dot32(y[at], w[2, :, cols])
            activated, slope = silu_parts(pre_gate)
            gg[at, cols] = (back * pre_up * slope).astype(jnp.bfloat16)
            gu[at, cols] = (back * activated).astype(jnp.bfloat16)
            hb[at, cols] = (activated * pre_up).astype(jnp.bfloat16)
    if first:
        own_grad[...] = dot32(gg[:rows], w[0], ((1,), (1,))) + dot32(gu[:rows], w[1], ((1,), (1,)))
    kept = outs[0].shape[1] * (2 if last else 1)
    half = kept // 2
    for i, (left, right) in enumerate(((x, gg), (x, gu), (y, hb))):
        if last:
            core = where_ref[1]
            for out, block in zip(outs, (core, 1 - core)):
                keep = pl.ds(pl.multiple_of(where_ref[0] * kept + block * half, half), half)
                term = dot32(left[:, keep], right[...], ((0,), (0,)))
                out[i] = term + total_in[i, pl.ds(pl.multiple_of(block * half, half), half)]
        else:
            keep = pl.ds(pl.multiple_of(where_ref[0] * kept, kept), kept)
            term = dot32(left[:, keep], right[...], ((0,), (0,)))
            outs[0][i] = term if first else term + total_in[i]


def common(where_at, kept, pieces, w, total, last=False):
    first = total is None
    n, rows, width = len(pieces), pieces[0].shape[0] // 2, pieces[0].shape[1]
    hidden_units = w.shape[2]
    shape, scratch = jax.ShapeDtypeStruct, pltpu.VMEM
    bf, f32 = jnp.bfloat16, jnp.float32
    out_shape = [shape((rows, width), f32)] if first else []
    if last:
        out_shape += [shape((3, kept // 2, hidden_units), f32)] * 2
    else:
        out_shape += [shape((3, kept, hidden_units), f32)]
    args = list(pieces) + [w] + ([] if first else [total])
    return pl.pallas_call(
        functools.partial(common_kernel, n, first, last),
        out_shape=out_shape,
        in_specs=[IN_SMEM] + [IN_VMEM] * len(args),
        out_specs=[IN_VMEM] * len(out_shape),
        scratch_shapes=[scratch((n * rows, width), bf)] * 2
        + [scratch((n * rows, hidden_units), bf)] * 3,
        cost_estimate=pl.CostEstimate(
            flops=6 * n * rows * hidden_units * (width + kept),
            bytes_accessed=2 * w.size + n * rows * width * 4,
            transcendentals=0,
        ),
        compiler_params=pltpu.CompilerParams(vmem_limit_bytes=24 * MIB),
        name="common",
    )(where_at, *args)


def weights_kernel(groups, *refs):
    saved, (own, sib, xs, sy, gg, gu, hb) = refs[: 5 * groups], refs[5 * groups :]
    for j in (1, 0):
        at = 0
        for g in range(groups):
            slots = saved[5 * g].shape[1]
            for i, into in enumerate((xs, sy, gg, gu, hb)):
                into[at : at + slots] = saved[5 * g + i][j]
            at += slots
        for i, (left, right) in enumerate(((xs, gg), (xs, gu), (sy, hb))):
            out = (own, sib)[j]
            out[i] = dot32(left[...], right[...], ((0,), (0,))).astype(out.dtype)


def weights(saved):
    groups = len(saved)
    flat = [a for group in saved for a in group]
    width, hidden_units = flat[0].shape[2], flat[2].shape[2]
    slots = sum(group[0].shape[1] for group in saved)
    bf, scratch = jnp.bfloat16, pltpu.VMEM
    return pl.pallas_call(
        functools.partial(weights_kernel, groups),
        out_shape=[
            jax.ShapeDtypeStruct((3, width, hidden_units), bf),
            jax.ShapeDtypeStruct((3, width, hidden_units), bf),
        ],
        in_specs=[IN_VMEM] * len(flat),
        out_specs=[IN_VMEM] * 2,
        scratch_shapes=[scratch((slots, width), bf)] * 2 + [scratch((slots, hidden_units), bf)] * 3,
        cost_estimate=pl.CostEstimate(
            flops=12 * slots * width * hidden_units,
            bytes_accessed=slots * (8 * width + 12 * hidden_units),
            transcendentals=0,
        ),
        compiler_params=pltpu.CompilerParams(vmem_limit_bytes=32 * MIB),
        name="weights",
    )(*flat)


def add_kernel(left, right, out):
    total = left[...].astype(jnp.float32) + right[...].astype(jnp.float32)
    out[...] = total.astype(out.dtype)


def add(left, right, dtype):
    block = pl.BlockSpec((1,) + left.shape[1:], lambda i: (i, 0, 0))
    return pl.pallas_call(
        add_kernel,
        grid=(left.shape[0],),
        out_shape=jax.ShapeDtypeStruct(left.shape, dtype),
        in_specs=[block] * 2,
        out_specs=block,
        compiler_params=pltpu.CompilerParams(vmem_limit_bytes=12 * MIB),
        name="add",
    )(left, right)


def join_kernel(left, right, out):
    rows = left.shape[0]
    out[:rows] = left[...]
    out[rows:] = right[...]


def join(left, right):
    rows, width = left.shape
    return pl.pallas_call(
        join_kernel,
        out_shape=jax.ShapeDtypeStruct((2 * rows, width), left.dtype),
        in_specs=[IN_VMEM] * 2,
        out_specs=IN_VMEM,
        compiler_params=pltpu.CompilerParams(vmem_limit_bytes=4 * MIB),
        name="join",
    )(left, right)


def finish_kernel(terms, ids_ref, *refs):
    sums, own_grad, (tokens_out, gates_out) = refs[:terms], refs[terms], refs[terms + 1 :]
    rows, top_count = ids_ref.shape
    total = sums[0][...].astype(jnp.float32)
    for ref in sums[1:]:
        total = total + ref[...].astype(jnp.float32)
    tokens_out[...] = (total[:rows] + own_grad[...]).astype(tokens_out.dtype)
    blocks = total.shape[1] // rows
    lines = [
        total[r : r + 1, b * rows : (b + 1) * rows]
        for r in range(rows, total.shape[0])
        for b in range(blocks)
    ]
    by_expert = jnp.concatenate(lines, axis=0).T
    expert = lax.broadcasted_iota(jnp.int32, by_expert.shape, 1)
    picked = [
        jnp.sum(jnp.where(ids_ref[:, k : k + 1] == expert, by_expert, 0.0), axis=1, keepdims=True)
        for k in range(top_count)
    ]
    gates_out[...] = jnp.concatenate(picked, axis=1).astype(gates_out.dtype)


def finish(expert_ids, sums, own_grad):
    rows, top_count = expert_ids.shape
    return pl.pallas_call(
        functools.partial(finish_kernel, len(sums)),
        out_shape=[
            jax.ShapeDtypeStruct(own_grad.shape, jnp.bfloat16),
            jax.ShapeDtypeStruct((rows, top_count), jnp.bfloat16),
        ],
        in_specs=[IN_VMEM] * (len(sums) + 2),
        out_specs=[IN_VMEM] * 2,
        compiler_params=pltpu.CompilerParams(vmem_limit_bytes=8 * MIB),
        name="finish",
    )(expert_ids, *sums, own_grad)


def shared_rows(tokens, cotangent, expert_ids, gate_weights, expert_weights, shared_weights):
    return shared_rows_body(
        tokens, cotangent, expert_ids, gate_weights, expert_weights, shared_weights
    )


def shared_rows_body(tokens, cotangent, expert_ids, gate_weights, expert_weights, shared_weights):
    rows, width = tokens.shape
    top_count = expert_ids.shape[1]
    data_count, expert_count = lax.axis_size("dp"), lax.axis_size("expert")
    devices = data_count * expert_count
    cap = capacity_of(rows, top_count, devices)
    planes = expert_count // 2
    bf, f32 = jnp.bfloat16, jnp.float32
    me_dp, me_ex = lax.axis_index("dp"), lax.axis_index("expert")
    routes = {
        "x": ("expert", [(e, e ^ 1) for e in range(expert_count)]),
        "+": ("expert", [(e, (e + 2) % expert_count) for e in range(expert_count)]),
        "-": ("expert", [(e, (e - 2) % expert_count) for e in range(expert_count)]),
        "--": ("expert", [(e, (e - 4) % expert_count) for e in range(expert_count)]),
        "y": ("dp", [(d, d ^ 2) for d in range(data_count)]),
        "core": ("dp", [(d, d ^ 1) for d in range(data_count)]),
    }

    def send(way, array):
        return lax.ppermute(array, *routes[way])

    w_own = expert_weights[0]
    own = join(tokens, cotangent)
    w_sib = send("core", w_own)

    c, x, y, d = [own] + [None] * 3, [None] * 4, [None] * 4, [None] * 4
    c[1] = send("+", c[0])
    c[2] = send("+", c[1])
    c[3] = send("-", c[0])
    for s in range(planes):
        x[s] = send("x", c[s])
        y[s] = send("y", c[s])
    d[0] = send("x", y[0])
    d[1] = send("+", d[0])
    d[2] = send("y", x[2])
    d[3] = send("-", d[0])

    matches = expert_ids[:, :, None] == jnp.arange(devices, dtype=jnp.int32)
    by_expert = jnp.sum(jnp.where(matches, gate_weights[:, :, None].astype(f32), 0.0), axis=1)
    by_expert = by_expert.T.astype(bf).reshape(data_count // 2, 2, expert_count, rows)
    outward = jnp.stack([by_expert, by_expert[:, ::-1]], axis=3).reshape(devices, 2, rows)
    inward = lax.all_to_all(outward, ("dp", "expert"), 0, 0, tiled=True)
    order = []
    for s in range(planes):
        plane = (me_ex // 2 + planes - s) % planes
        for dy, dx in ((0, 0), (0, 1), (1, 0), (1, 1)):
            source = (me_dp ^ (2 * dy)) * expert_count + plane * 2 + (me_ex % 2 ^ dx)
            order.append(source)
    pick = jnp.stack(order)[:, None] == jnp.arange(devices, dtype=jnp.int32)[None, :]
    pick = pick.astype(bf)
    gates = jnp.dot(pick, inward.reshape(devices, 2 * rows), preferred_element_type=f32)
    gates = gates.reshape(planes, 4, 2, rows)

    extra = 8 * (-(-devices * rows // (8 * width)))
    blocks = width // rows
    me = me_dp * expert_count + me_ex
    sibling = (me_dp ^ 1) * expert_count + me_ex
    at = jnp.stack([me // blocks, me % blocks, sibling // blocks, sibling % blocks])
    at = at.astype(jnp.int32)
    part, saved = [None] * 4, [None] * 4
    for s in (0, 2, 1, 3):
        part[s], saved[s] = route(s, cap, extra, at, gates, (c[s], x[s], y[s], d[s]), w_own, w_sib)
    pc, px, py, pd = zip(*part)

    where_at = jnp.stack([me_dp // 2, me_dp % 2]).astype(jnp.int32)
    kept = 2 * (width // data_count)
    pieces = (c[0], x[0], y[0], c[1])
    shared_grad, total = common(where_at, kept, pieces, shared_weights, None)
    pieces = (d[0], y[1], c[2], y[2])
    (total,) = common(where_at, kept, pieces, shared_weights, total)
    pieces = (x[2], c[3], x[1], d[1], d[2], x[3], y[3], d[3])
    mine, other = common(where_at, kept, pieces, shared_weights, total, last=True)

    def plus(*terms):
        total = terms[0].astype(f32)
        for term in terms[1:]:
            total = total + term.astype(f32)
        return total

    def home_x(array):
        return send("x", array.astype(bf))

    def home_y(array):
        return send("y", array.astype(bf))

    x2 = plus(px[2], send("y", pd[2]))
    c2 = plus(pc[2], home_x(x2), home_y(py[2]))
    c1 = plus(pc[1], home_x(px[1]), home_y(py[1]))
    c3 = plus(pc[3], home_x(px[3]), home_y(py[3]))
    d0 = plus(pd[0], send("-", pd[1]), send("+", pd[3]))
    y0 = plus(py[0], send("x", d0.astype(bf)))
    sums = (pc[0], home_x(px[0]), home_y(y0))
    sums += (send("-", c1.astype(bf)), send("+", c3.astype(bf)))
    sums += (send("--", c2.astype(bf)),)
    grad_tokens, grad_gates = finish(expert_ids, sums, shared_grad)

    mine_experts, for_sib = weights(saved)
    came = send("core", for_sib)
    came_shared = send("core", other)
    grad_experts = add(mine_experts, came, bf)[None]
    grad_shared = add(mine, came_shared, f32)
    return (grad_tokens, grad_gates, grad_experts, grad_shared)


def solution(mesh):
    placed = (
        P(("dp", "expert"), None),
        P(("dp", "expert"), None),
        P(("dp", "expert"), None),
        P(("dp", "expert"), None),
        P(("dp", "expert"), None, None, None),
        P(),
    )
    share = mesh.shape["dp"] == 4 and mesh.shape["expert"] == 8
    return jax.shard_map(
        shared_rows if share else shards,
        mesh=mesh,
        in_specs=placed,
        out_specs=(
            P(("dp", "expert"), None),
            P(("dp", "expert"), None),
            P(("dp", "expert"), None, None, None),
            P(None, "dp", None),
        ),
        check_vma=False,
    )
```

```python
import functools

import jax
import jax.numpy as jnp
from jax import lax
from jax.experimental import pallas as pl
from jax.experimental.pallas import tpu as pltpu
from jax.sharding import PartitionSpec as P


def silu_parts(pre):
    sigma = jax.nn.sigmoid(pre)
    return (pre * sigma, sigma * (1.0 + pre * (1.0 - sigma)))


def contract_rows(left, right):
    return lax.dot_general(
        left, right, (((0,), (0,)), ((), ())), preferred_element_type=jnp.float32
    )


def expert_grads(inputs, upstream, scales, weight):
    hidden_units = weight.shape[2]
    paired = jnp.concatenate([weight[0], weight[1]], axis=1)
    gate_up = jnp.dot(inputs, paired, preferred_element_type=jnp.float32)
    pre_gate = gate_up[:, :hidden_units]
    pre_up = gate_up[:, hidden_units:]
    back = jnp.dot(upstream, weight[2], preferred_element_type=jnp.float32)
    activated, slope = silu_parts(pre_gate)
    hidden = activated * pre_up
    gate_grad = jnp.sum(hidden * back, axis=1)
    scaled = scales[:, None] * back
    grad_gate_in = (scaled * pre_up * slope).astype(jnp.bfloat16)
    grad_up_in = (scaled * activated).astype(jnp.bfloat16)
    both = jnp.concatenate([grad_gate_in, grad_up_in], axis=1)
    input_grad = lax.dot_general(
        both, paired, (((1,), (1,)), ((), ())), preferred_element_type=jnp.float32
    )
    hidden_b = hidden.astype(jnp.bfloat16)
    scaled_up = (scales[:, None] * upstream.astype(jnp.float32)).astype(jnp.bfloat16)
    return (input_grad, gate_grad, grad_gate_in, grad_up_in, hidden_b, scaled_up)


def weight_terms(inputs, grad_gate_in, grad_up_in, scaled_up, hidden_b):
    return jnp.stack(
        [
            contract_rows(inputs, grad_gate_in),
            contract_rows(inputs, grad_up_in),
            contract_rows(scaled_up, hidden_b),
        ],
        axis=0,
    )


def capacity_of(tok_rows, top_count, devices):
    return max(2, (6 * tok_rows * top_count + 5 * devices - 1) // (5 * devices))


def shards(tokens, cotangent, expert_ids, gate_weights, expert_weights, shared_weights):
    tok_rows, model_width = tokens.shape
    top_count = expert_ids.shape[1]
    data_count = lax.axis_size("dp")
    expert_count = lax.axis_size("expert")
    devices = data_count * expert_count
    capacity = capacity_of(tok_rows, top_count, devices)
    slot_total = devices * capacity
    pair_count = tok_rows * top_count
    row_ids = jnp.arange(tok_rows, dtype=jnp.int32)
    earlier_mask = (row_ids[:, None] > row_ids[None, :]).astype(jnp.bfloat16)
    padded_tokens = jnp.concatenate([tokens, jnp.zeros((1, model_width), jnp.bfloat16)], axis=0)
    padded_cotangent = jnp.concatenate(
        [cotangent, jnp.zeros((1, model_width), jnp.bfloat16)], axis=0
    )
    matches = expert_ids[:, :, None] == jnp.arange(devices, dtype=jnp.int32)
    per_token = jnp.sum(matches, axis=1).astype(jnp.bfloat16)
    before = jnp.dot(earlier_mask, per_token, preferred_element_type=jnp.float32)
    slot_index = jnp.sum(jnp.where(matches, before[:, None, :], 0.0), axis=2).astype(jnp.int32)
    position = expert_ids * capacity + slot_index
    slot_table = (
        jnp.full((slot_total,), pair_count, jnp.int32)
        .at[position.reshape(-1)]
        .set(jnp.arange(pair_count, dtype=jnp.int32))
    )
    token_index = slot_table // top_count
    padded_gates = jnp.concatenate(
        [gate_weights.reshape(-1), jnp.zeros((1,), jnp.bfloat16)], axis=0
    )
    send_tokens = padded_tokens[token_index].reshape(
        data_count, expert_count, capacity, model_width
    )
    send_cotangent = padded_cotangent[token_index].reshape(
        data_count, expert_count, capacity, model_width
    )
    send_gates = padded_gates[slot_table].reshape(data_count, expert_count, capacity)
    arrived = (
        lax.all_to_all(
            lax.all_to_all(send_tokens, "dp", split_axis=0, concat_axis=0, tiled=True),
            "expert",
            split_axis=1,
            concat_axis=1,
            tiled=True,
        ),
        lax.all_to_all(
            lax.all_to_all(send_cotangent, "dp", split_axis=0, concat_axis=0, tiled=True),
            "expert",
            split_axis=1,
            concat_axis=1,
            tiled=True,
        ),
        lax.all_to_all(
            lax.all_to_all(send_gates, "dp", split_axis=0, concat_axis=0, tiled=True),
            "expert",
            split_axis=1,
            concat_axis=1,
            tiled=True,
        ),
    )
    arrived_tokens = arrived[0].reshape(slot_total, model_width)
    routed = expert_grads(
        arrived_tokens,
        arrived[1].reshape(slot_total, model_width),
        arrived[2].reshape(slot_total).astype(jnp.float32),
        expert_weights[0],
    )
    grad_experts = weight_terms(arrived_tokens, routed[2], routed[3], routed[5], routed[4]).astype(
        jnp.bfloat16
    )[None]
    outgoing_input = (
        routed[0].astype(jnp.bfloat16).reshape(data_count, expert_count, capacity, model_width)
    )
    outgoing_gate = routed[1].astype(jnp.bfloat16).reshape(data_count, expert_count, capacity)
    returned = (
        lax.all_to_all(
            lax.all_to_all(outgoing_input, "dp", split_axis=0, concat_axis=0, tiled=True),
            "expert",
            split_axis=1,
            concat_axis=1,
            tiled=True,
        ),
        lax.all_to_all(
            lax.all_to_all(outgoing_gate, "dp", split_axis=0, concat_axis=0, tiled=True),
            "expert",
            split_axis=1,
            concat_axis=1,
            tiled=True,
        ),
    )
    flat_back = returned[0].reshape(slot_total, model_width)
    routed_sum = jnp.sum(flat_back[position].astype(jnp.float32), axis=1)
    grad_gates = returned[1].reshape(slot_total)[position]
    shared = expert_grads(tokens, cotangent, jnp.ones((tok_rows,), jnp.float32), shared_weights)
    grad_tokens = (routed_sum + shared[0]).astype(jnp.bfloat16)
    kept_rows = model_width // data_count
    shared_units = shared_weights.shape[2]
    upstream_cols = shared[5]
    kept = lax.psum_scatter(
        jnp.concatenate(
            [
                contract_rows(tokens, shared[2]),
                contract_rows(tokens, shared[3]),
                contract_rows(upstream_cols, shared[4]),
            ],
            axis=1,
        ),
        "dp",
        scatter_dimension=0,
        tiled=True,
    )
    totals = lax.psum(kept, "expert")
    grad_shared = jnp.transpose(totals.reshape(kept_rows, 3, shared_units), (1, 0, 2))
    return (grad_tokens, grad_gates, grad_experts, grad_shared)


def strict_upper(rows):
    r = lax.broadcasted_iota(jnp.int32, (rows, rows), 0)
    c = lax.broadcasted_iota(jnp.int32, (rows, rows), 1)
    return (r < c).astype(jnp.bfloat16)


def dot32(left, right, dims=((1,), (0,))):
    return lax.dot_general(left, right, (dims, ((), ())), preferred_element_type=jnp.float32)


def route_kernel(group, n, cap, at_ref, gates_ref, *refs):
    pieces, w_refs = refs[:n], refs[n : n + 2]
    parts = refs[n + 2 : 2 * n + 2]
    xs, sy, gg, gu, hb, onehot, yslot, ig = refs[2 * n + 2 :]
    rows, width = gates_ref.shape[3], pieces[0].shape[1]
    gates = jnp.concatenate([gates_ref[s] for s in group], axis=0)
    named = jnp.where(gates > 0, 1.0, 0.0)
    before = dot32(named.reshape(2 * n, rows).astype(jnp.bfloat16), strict_upper(rows))
    before = before.reshape(n, 2, rows)
    slot = lax.broadcasted_iota(jnp.int32, (cap, rows), 0).astype(jnp.float32)
    scales = [[], []]
    for p in range(n):
        for j in range(2):
            hit = (before[p, j][None, :] == slot) & (named[p, j][None, :] > 0)
            hit = jnp.where(hit, 1.0, 0.0)
            onehot[p, j * cap : (j + 1) * cap] = hit.astype(jnp.bfloat16)
            scales[j].append(jnp.sum(hit * gates[p, j][None, :], axis=1, keepdims=True))
        picked_x = dot32(onehot[p], pieces[p][:rows]).astype(jnp.bfloat16)
        picked_y = dot32(onehot[p], pieces[p][rows:])
        for j in range(2):
            here = slice(p * cap, (p + 1) * cap)
            there = slice(j * cap, (j + 1) * cap)
            xs[j, here] = picked_x[there]
            yslot[j, here] = picked_y[there].astype(jnp.bfloat16)
            sy[j, here] = (picked_y[there] * scales[j][p]).astype(jnp.bfloat16)
    hidden_units = w_refs[0].shape[2]
    tile = min(256, hidden_units)
    grads = []
    for j, w in enumerate(w_refs):
        scale = jnp.concatenate(scales[j], axis=0)
        gate_grad = jnp.zeros((n * cap, 1), jnp.float32)
        for f in range(0, hidden_units, tile):
            cols = slice(f, f + tile)
            pre_gate = dot32(xs[j], w[0, :, cols])
            pre_up = dot32(xs[j], w[1, :, cols])
            back = dot32(yslot[j], w[2, :, cols])
            activated, slope = silu_parts(pre_gate)
            hidden = activated * pre_up
            gate_grad += jnp.sum(hidden * back, axis=1, keepdims=True)
            scaled = scale * back
            gg[j, :, cols] = (scaled * pre_up * slope).astype(jnp.bfloat16)
            gu[j, :, cols] = (scaled * activated).astype(jnp.bfloat16)
            hb[j, :, cols] = hidden.astype(jnp.bfloat16)
        ig[j] = (
            dot32(gg[j], w[0], ((1,), (1,))) + dot32(gu[j], w[1], ((1,), (1,)))
        ).astype(jnp.bfloat16)
        grads.append(gate_grad)
    extra = parts[0].shape[0] - rows
    row = lax.broadcasted_iota(jnp.int32, (extra, width), 0)
    block = lax.broadcasted_iota(jnp.int32, (extra, width), 1) // rows
    for p in range(n):
        tail = jnp.zeros((extra, width), jnp.float32)
        for j in range(2):
            here = slice(p * cap, (p + 1) * cap)
            hit = onehot[p, j * cap : (j + 1) * cap].astype(jnp.float32)
            line = jnp.sum(hit * grads[j][here], axis=0, keepdims=True)
            line = jnp.concatenate([line] * (width // rows), axis=1)
            mine = (row == at_ref[2 * j]) & (block == at_ref[2 * j + 1])
            tail = tail + jnp.where(mine, line, 0.0)
        both = jnp.concatenate([ig[j, here] for j in range(2)], axis=0)
        parts[p][:rows] = dot32(onehot[p], both, ((0,), (0,))).astype(parts[p].dtype)
        parts[p][rows:] = tail.astype(jnp.bfloat16).astype(parts[p].dtype)


MIB = 1024 * 1024
IN_SMEM = pl.BlockSpec(memory_space=pltpu.SMEM)
IN_VMEM = pl.BlockSpec(memory_space=pltpu.VMEM)


def route(group, cap, extra, at, gates, pieces, w_own, w_sib):
    n, rows, width = len(pieces), gates.shape[3], pieces[0].shape[1]
    hidden_units = w_own.shape[2]
    slots = n * cap
    shape, scratch = jax.ShapeDtypeStruct, pltpu.VMEM
    bf = jnp.bfloat16
    kinds = [bf if p % 4 else jnp.float32 for p in range(n)]
    out_shape = [shape((rows + extra, width), kind) for kind in kinds]
    out_shape += [shape((2, slots, width), bf)] * 2 + [shape((2, slots, hidden_units), bf)] * 3
    outs = pl.pallas_call(
        functools.partial(route_kernel, group, n, cap),
        out_shape=out_shape,
        in_specs=[IN_SMEM] + [IN_VMEM] * (n + 3),
        out_specs=[IN_VMEM] * (n + 5),
        scratch_shapes=[
            scratch((n, 2 * cap, rows), bf),
            scratch((2, slots, width), bf),
            scratch((2, slots, width), bf),
        ],
        cost_estimate=pl.CostEstimate(
            flops=20 * slots * width * hidden_units,
            bytes_accessed=4 * w_own.size + 16 * slots * width,
            transcendentals=0,
        ),
        compiler_params=pltpu.CompilerParams(vmem_limit_bytes=14 * MIB),
        name="route",
    )(at, gates, *pieces, w_own, w_sib)
    return outs[:n], outs[n:]


def common_kernel(n, first, last, where_ref, *refs):
    pieces, w, refs = refs[:n], refs[n], refs[n + 1 :]
    (own_grad,), refs = (refs[:1], refs[1:]) if first else ((None,), refs)
    (total_in,), refs = ((None,), refs) if first else (refs[:1], refs[1:])
    outs, (x, y, gg, gu, hb) = refs[:-5], refs[-5:]
    rows = pieces[0].shape[0] // 2
    for p in range(n):
        x[p * rows : (p + 1) * rows] = pieces[p][:rows]
        y[p * rows : (p + 1) * rows] = pieces[p][rows:]
    hidden_units = w.shape[2]
    tile = min(256, hidden_units)
    chunk = 4 * rows
    for r in range(0, n * rows, chunk):
        at = slice(r, min(r + chunk, n * rows))
        for f in range(0, hidden_units, tile):
            cols = slice(f, f + tile)
            pre_gate = dot32(x[at], w[0, :, cols])
            pre_up = dot32(x[at], w[1, :, cols])
            back = dot32(y[at], w[2, :, cols])
            activated, slope = silu_parts(pre_gate)
            gg[at, cols] = (back * pre_up * slope).astype(jnp.bfloat16)
            gu[at, cols] = (back * activated).astype(jnp.bfloat16)
            hb[at, cols] = (activated * pre_up).astype(jnp.bfloat16)
    if first:
        own_grad[...] = dot32(gg[:rows], w[0], ((1,), (1,))) + dot32(gu[:rows], w[1], ((1,), (1,)))
    kept = outs[0].shape[1] * (2 if last else 1)
    half = kept // 2
    for i, (left, right) in enumerate(((x, gg), (x, gu), (y, hb))):
        if last:
            core = where_ref[1]
            for out, block in zip(outs, (core, 1 - core)):
                keep = pl.ds(pl.multiple_of(where_ref[0] * kept + block * half, half), half)
                term = dot32(left[:, keep], right[...], ((0,), (0,)))
                term = term + total_in[i, pl.ds(pl.multiple_of(block * half, half), half)]
                out[i] = term.astype(out.dtype)
        else:
            keep = pl.ds(pl.multiple_of(where_ref[0] * kept, kept), kept)
            term = dot32(left[:, keep], right[...], ((0,), (0,)))
            outs[0][i] = term if first else term + total_in[i]


def common(where_at, kept, pieces, w, total, last=False):
    first = total is None
    n, rows, width = len(pieces), pieces[0].shape[0] // 2, pieces[0].shape[1]
    hidden_units = w.shape[2]
    shape, scratch = jax.ShapeDtypeStruct, pltpu.VMEM
    bf, f32 = jnp.bfloat16, jnp.float32
    out_shape = [shape((rows, width), f32)] if first else []
    if last:
        out_shape += [shape((3, kept // 2, hidden_units), dtype) for dtype in (f32, bf)]
    else:
        out_shape += [shape((3, kept, hidden_units), f32)]
    args = list(pieces) + [w] + ([] if first else [total])
    return pl.pallas_call(
        functools.partial(common_kernel, n, first, last),
        out_shape=out_shape,
        in_specs=[IN_SMEM] + [IN_VMEM] * len(args),
        out_specs=[IN_VMEM] * len(out_shape),
        scratch_shapes=[scratch((n * rows, width), bf)] * 2
        + [scratch((n * rows, hidden_units), bf)] * 3,
        cost_estimate=pl.CostEstimate(
            flops=6 * n * rows * hidden_units * (width + kept),
            bytes_accessed=2 * w.size + n * rows * width * 4,
            transcendentals=0,
        ),
        compiler_params=pltpu.CompilerParams(vmem_limit_bytes=14 * MIB),
        name="common",
    )(where_at, *args)


def weights_kernel(groups, *refs):
    saved, (own, sib, xs, sy, gg, gu, hb) = refs[: 5 * groups], refs[5 * groups :]
    for j in (1, 0):
        at = 0
        for g in range(groups):
            slots = saved[5 * g].shape[1]
            for i, into in enumerate((xs, sy, gg, gu, hb)):
                into[at : at + slots] = saved[5 * g + i][j]
            at += slots
        for i, (left, right) in enumerate(((xs, gg), (xs, gu), (sy, hb))):
            out = (own, sib)[j]
            out[i] = dot32(left[...], right[...], ((0,), (0,))).astype(out.dtype)


def weights(saved):
    groups = len(saved)
    flat = [a for group in saved for a in group]
    width, hidden_units = flat[0].shape[2], flat[2].shape[2]
    slots = sum(group[0].shape[1] for group in saved)
    bf, scratch = jnp.bfloat16, pltpu.VMEM
    return pl.pallas_call(
        functools.partial(weights_kernel, groups),
        out_shape=[
            jax.ShapeDtypeStruct((3, width, hidden_units), bf),
            jax.ShapeDtypeStruct((3, width, hidden_units), bf),
        ],
        in_specs=[IN_VMEM] * len(flat),
        out_specs=[IN_VMEM] * 2,
        scratch_shapes=[scratch((slots, width), bf)] * 2 + [scratch((slots, hidden_units), bf)] * 3,
        cost_estimate=pl.CostEstimate(
            flops=12 * slots * width * hidden_units,
            bytes_accessed=slots * (8 * width + 12 * hidden_units),
            transcendentals=0,
        ),
        compiler_params=pltpu.CompilerParams(vmem_limit_bytes=18 * MIB),
        name="weights",
    )(*flat)


def sums_kernel(e_mine, s_mine, e_came, s_came, e_out, s_out, *scratch):
    e_in, s_in, e_res, s_res, sem_in, sem_out = scratch
    count = e_mine.shape[0]
    parts = [(e_mine, e_came, e_in, e_res, e_out, i, i) for i in range(count)]
    parts += [(s_mine, s_came, s_in, s_res, s_out, i, count + i) for i in range(count)]
    bring = [
        pltpu.make_async_copy(came.at[i], into.at[i], sem_in.at[k])
        for _, came, into, _, _, i, k in parts
    ]
    for copy in bring:
        copy.start()
    sends = []
    for (mine, _, into, res, out, i, k), copy in zip(parts, bring):
        copy.wait()
        res[i] = (mine[i].astype(jnp.float32) + into[i].astype(jnp.float32)).astype(res.dtype)
        sends.append(pltpu.make_async_copy(res.at[i], out.at[i], sem_out.at[k]))
        sends[-1].start()
    for copy in sends:
        copy.wait()


def last_sums(e_mine, s_mine, e_came, s_came):
    shape, scratch, dma = jax.ShapeDtypeStruct, pltpu.VMEM, pltpu.SemaphoreType.DMA
    bf, f32 = jnp.bfloat16, jnp.float32
    count = e_mine.shape[0]
    in_place = pl.BlockSpec(memory_space=pl.ANY)
    return pl.pallas_call(
        sums_kernel,
        out_shape=[shape(e_mine.shape, bf), shape(s_mine.shape, f32)],
        in_specs=[IN_VMEM] * 2 + [in_place] * 2,
        out_specs=[in_place] * 2,
        scratch_shapes=[scratch(e_came.shape, bf), scratch(s_came.shape, bf)]
        + [scratch(e_mine.shape, bf), scratch(s_mine.shape, f32)]
        + [dma((2 * count,)), dma((2 * count,))],
        compiler_params=pltpu.CompilerParams(vmem_limit_bytes=16 * MIB),
        name="sums",
    )(e_mine, s_mine, e_came, s_came)


def hold_kernel(array, out, sem):
    copy = pltpu.make_async_copy(array, out, sem.at[0])
    copy.start()
    copy.wait()


def hold(array):
    return pl.pallas_call(
        hold_kernel,
        out_shape=jax.ShapeDtypeStruct(array.shape, array.dtype),
        in_specs=[pl.BlockSpec(memory_space=pltpu.HBM)],
        out_specs=IN_VMEM,
        scratch_shapes=[pltpu.SemaphoreType.DMA((1,))],
        compiler_params=pltpu.CompilerParams(vmem_limit_bytes=4 * MIB),
        name="hold",
    )(array)


def join_kernel(left, right, out, sem):
    rows = left.shape[0]
    copies = [
        pltpu.make_async_copy(left, out.at[pl.ds(0, rows)], sem.at[0]),
        pltpu.make_async_copy(right, out.at[pl.ds(rows, rows)], sem.at[1]),
    ]
    for copy in copies:
        copy.start()
    for copy in copies:
        copy.wait()


def join(left, right):
    rows, width = left.shape
    return pl.pallas_call(
        join_kernel,
        out_shape=jax.ShapeDtypeStruct((2 * rows, width), left.dtype),
        in_specs=[pl.BlockSpec(memory_space=pltpu.HBM)] * 2,
        out_specs=IN_VMEM,
        scratch_shapes=[pltpu.SemaphoreType.DMA((2,))],
        compiler_params=pltpu.CompilerParams(vmem_limit_bytes=60 * MIB),
        name="join",
    )(left, right)


def finish_kernel(terms, ids_ref, *refs):
    sums, own_grad, (tokens_out, gates_out) = refs[:terms], refs[terms], refs[terms + 1 :]
    top_count, rows = ids_ref.shape
    total = sums[0][...].astype(jnp.float32)
    for ref in sums[1:]:
        total = total + ref[...].astype(jnp.float32)
    tokens_out[...] = (total[:rows] + own_grad[...]).astype(tokens_out.dtype)
    blocks = total.shape[1] // rows
    by_expert = jnp.concatenate(
        [
            total[r : r + 1, b * rows : (b + 1) * rows]
            for r in range(rows, total.shape[0])
            for b in range(blocks)
        ],
        axis=0,
    )
    expert = lax.broadcasted_iota(jnp.int32, by_expert.shape, 0)
    picked = [
        jnp.sum(jnp.where(ids_ref[k : k + 1] == expert, by_expert, 0.0), axis=0, keepdims=True)
        for k in range(top_count)
    ]
    gates_out[...] = jnp.concatenate(picked, axis=0).astype(gates_out.dtype)


def finish(expert_ids, sums, own_grad):
    rows, top_count = expert_ids.shape
    tokens, gates = pl.pallas_call(
        functools.partial(finish_kernel, len(sums)),
        out_shape=[
            jax.ShapeDtypeStruct(own_grad.shape, jnp.bfloat16),
            jax.ShapeDtypeStruct((top_count, rows), jnp.bfloat16),
        ],
        in_specs=[IN_VMEM] * (len(sums) + 2),
        out_specs=[IN_VMEM] * 2,
        compiler_params=pltpu.CompilerParams(vmem_limit_bytes=8 * MIB),
        name="finish",
    )(expert_ids.T, *sums, own_grad)
    return tokens, gates.T


def shared_rows(tokens, cotangent, expert_ids, gate_weights, expert_weights, shared_weights):
    return shared_rows_body(
        tokens, cotangent, expert_ids, gate_weights, expert_weights, shared_weights
    )


def shared_rows_body(tokens, cotangent, expert_ids, gate_weights, expert_weights, shared_weights):
    rows, width = tokens.shape
    top_count = expert_ids.shape[1]
    data_count, expert_count = lax.axis_size("dp"), lax.axis_size("expert")
    devices = data_count * expert_count
    cap = capacity_of(rows, top_count, devices)
    planes = expert_count // 2
    bf, f32 = jnp.bfloat16, jnp.float32
    me_dp, me_ex = lax.axis_index("dp"), lax.axis_index("expert")
    routes = {
        "x": ("expert", [(e, e ^ 1) for e in range(expert_count)]),
        "+": ("expert", [(e, (e + 2) % expert_count) for e in range(expert_count)]),
        "-": ("expert", [(e, (e - 2) % expert_count) for e in range(expert_count)]),
        "y": ("dp", [(d, d ^ 2) for d in range(data_count)]),
        "core": ("dp", [(d, d ^ 1) for d in range(data_count)]),
    }

    def send(way, array):
        return lax.ppermute(array, *routes[way])

    w_own = expert_weights[0]
    own = join(tokens, cotangent)
    w_sib = send("core", w_own)
    w_sib = hold(w_sib)

    c, x, y, d = [own] + [None] * 3, [None] * 4, [None] * 4, [None] * 4
    c[1] = send("+", c[0])
    c[2] = send("+", c[1])
    c[3] = send("-", c[0])
    for s in range(planes):
        x[s] = send("x", c[s])
        y[s] = send("y", c[s])
    d[0] = send("x", y[0])
    d[1] = send("+", d[0])
    d[2] = send("y", x[2])
    d[3] = send("x", y[3])

    matches = expert_ids[:, :, None] == jnp.arange(devices, dtype=jnp.int32)
    by_expert = jnp.sum(jnp.where(matches, gate_weights[:, :, None].astype(f32), 0.0), axis=1)
    by_expert = by_expert.T.astype(bf).reshape(data_count // 2, 2, expert_count, rows)
    outward = jnp.stack([by_expert, by_expert[:, ::-1]], axis=3).reshape(devices, 2, rows)
    inward = lax.all_to_all(outward, ("dp", "expert"), 0, 0, tiled=True)
    order = []
    for s in range(planes):
        plane = (me_ex // 2 + planes - s) % planes
        for dy, dx in ((0, 0), (0, 1), (1, 0), (1, 1)):
            source = (me_dp ^ (2 * dy)) * expert_count + plane * 2 + (me_ex % 2 ^ dx)
            order.append(source)
    pick = jnp.stack(order)[:, None] == jnp.arange(devices, dtype=jnp.int32)[None, :]
    pick = pick.astype(bf)
    gates = jnp.dot(pick, inward.reshape(devices, 2 * rows), preferred_element_type=f32)
    gates = gates.reshape(planes, 4, 2, rows)

    extra = 8 * (-(-devices * rows // (8 * width)))
    blocks = width // rows
    me = me_dp * expert_count + me_ex
    sibling = (me_dp ^ 1) * expert_count + me_ex
    at = jnp.stack([me // blocks, me % blocks, sibling // blocks, sibling % blocks])
    at = at.astype(jnp.int32)
    part, saved = [None] * 4, []
    for group in ((0,), (2,), (1, 3)):
        pieces = [piece for s in group for piece in (c[s], x[s], y[s], d[s])]
        sums, keep = route(group, cap, extra, at, gates, pieces, w_own, w_sib)
        saved.append(keep)
        for i, s in enumerate(group):
            part[s] = sums[4 * i : 4 * i + 4]
    pc, px, py, pd = zip(*part)

    where_at = jnp.stack([me_dp // 2, me_dp % 2]).astype(jnp.int32)
    kept = 2 * (width // data_count)
    pieces = (c[0], x[0], y[0], c[1])
    shared_grad, total = common(where_at, kept, pieces, shared_weights, None)
    pieces = (d[0], y[1], x[1], c[2])
    (total,) = common(where_at, kept, pieces, shared_weights, total)
    pieces = (c[3], x[2], y[2])
    (total,) = common(where_at, kept, pieces, shared_weights, total)
    pieces = (d[1], x[3], y[3])
    (total,) = common(where_at, kept, pieces, shared_weights, total)
    pieces = (d[2], d[3])
    mine, other = common(where_at, kept, pieces, shared_weights, total, last=True)

    def plus(*terms):
        total = terms[0].astype(f32)
        for term in terms[1:]:
            total = total + term.astype(f32)
        return total

    def home_x(array):
        return send("x", array.astype(bf))

    def home_y(array):
        return send("y", array.astype(bf))

    part_x, part_y = list(px), list(py)
    for s in range(planes):
        if s in (0, 3):
            part_y[s] = plus(py[s], send("x", pd[s]))
        else:
            part_x[s] = plus(px[s], send("y", pd[s]))
    arrived = [(pc[s], home_x(part_x[s]), home_y(part_y[s])) for s in range(planes)]
    c3 = arrived[3] + (send("+", plus(*arrived[2]).astype(bf)),)
    sums = arrived[0] + (send("-", plus(*arrived[1]).astype(bf)),)
    sums += (send("+", plus(*c3).astype(bf)),)
    grad_tokens, grad_gates = finish(expert_ids, sums, shared_grad)

    mine_experts, for_sib = weights(saved)
    came = send("core", for_sib)
    came_shared = send("core", other)
    grad_experts, grad_shared = last_sums(mine_experts, mine, came, came_shared)
    grad_experts = grad_experts[None]
    return (grad_tokens, grad_gates, grad_experts, grad_shared)


def solution(mesh):
    placed = (
        P(("dp", "expert"), None),
        P(("dp", "expert"), None),
        P(("dp", "expert"), None),
        P(("dp", "expert"), None),
        P(("dp", "expert"), None, None, None),
        P(),
    )
    share = mesh.shape["dp"] == 4 and mesh.shape["expert"] == 8
    return jax.shard_map(
        shared_rows if share else shards,
        mesh=mesh,
        in_specs=placed,
        out_specs=(
            P(("dp", "expert"), None),
            P(("dp", "expert"), None),
            P(("dp", "expert"), None, None, None),
            P(None, "dp", None),
        ),
        check_vma=False,
    )
```

```python
import functools

import jax
import jax.numpy as jnp
from jax import lax
from jax.experimental import pallas as pl
from jax.experimental.pallas import tpu as pltpu
from jax.sharding import PartitionSpec as P


def silu_parts(pre):
    sigma = jax.nn.sigmoid(pre)
    return (pre * sigma, sigma * (1.0 + pre * (1.0 - sigma)))


def contract_rows(left, right):
    return lax.dot_general(
        left, right, (((0,), (0,)), ((), ())), preferred_element_type=jnp.float32
    )


def expert_grads(inputs, upstream, scales, weight):
    hidden_units = weight.shape[2]
    paired = jnp.concatenate([weight[0], weight[1]], axis=1)
    gate_up = jnp.dot(inputs, paired, preferred_element_type=jnp.float32)
    pre_gate = gate_up[:, :hidden_units]
    pre_up = gate_up[:, hidden_units:]
    back = jnp.dot(upstream, weight[2], preferred_element_type=jnp.float32)
    activated, slope = silu_parts(pre_gate)
    hidden = activated * pre_up
    gate_grad = jnp.sum(hidden * back, axis=1)
    scaled = scales[:, None] * back
    grad_gate_in = (scaled * pre_up * slope).astype(jnp.bfloat16)
    grad_up_in = (scaled * activated).astype(jnp.bfloat16)
    both = jnp.concatenate([grad_gate_in, grad_up_in], axis=1)
    input_grad = lax.dot_general(
        both, paired, (((1,), (1,)), ((), ())), preferred_element_type=jnp.float32
    )
    hidden_b = hidden.astype(jnp.bfloat16)
    scaled_up = (scales[:, None] * upstream.astype(jnp.float32)).astype(jnp.bfloat16)
    return (input_grad, gate_grad, grad_gate_in, grad_up_in, hidden_b, scaled_up)


def weight_terms(inputs, grad_gate_in, grad_up_in, scaled_up, hidden_b):
    return jnp.stack(
        [
            contract_rows(inputs, grad_gate_in),
            contract_rows(inputs, grad_up_in),
            contract_rows(scaled_up, hidden_b),
        ],
        axis=0,
    )


def capacity_of(tok_rows, top_count, devices):
    return max(2, (6 * tok_rows * top_count + 5 * devices - 1) // (5 * devices))


def shards(tokens, cotangent, expert_ids, gate_weights, expert_weights, shared_weights):
    tok_rows, model_width = tokens.shape
    top_count = expert_ids.shape[1]
    data_count = lax.axis_size("dp")
    expert_count = lax.axis_size("expert")
    devices = data_count * expert_count
    capacity = capacity_of(tok_rows, top_count, devices)
    slot_total = devices * capacity
    pair_count = tok_rows * top_count
    row_ids = jnp.arange(tok_rows, dtype=jnp.int32)
    earlier_mask = (row_ids[:, None] > row_ids[None, :]).astype(jnp.bfloat16)
    padded_tokens = jnp.concatenate([tokens, jnp.zeros((1, model_width), jnp.bfloat16)], axis=0)
    padded_cotangent = jnp.concatenate(
        [cotangent, jnp.zeros((1, model_width), jnp.bfloat16)], axis=0
    )
    matches = expert_ids[:, :, None] == jnp.arange(devices, dtype=jnp.int32)
    per_token = jnp.sum(matches, axis=1).astype(jnp.bfloat16)
    before = jnp.dot(earlier_mask, per_token, preferred_element_type=jnp.float32)
    slot_index = jnp.sum(jnp.where(matches, before[:, None, :], 0.0), axis=2).astype(jnp.int32)
    position = expert_ids * capacity + slot_index
    slot_table = (
        jnp.full((slot_total,), pair_count, jnp.int32)
        .at[position.reshape(-1)]
        .set(jnp.arange(pair_count, dtype=jnp.int32))
    )
    token_index = slot_table // top_count
    padded_gates = jnp.concatenate(
        [gate_weights.reshape(-1), jnp.zeros((1,), jnp.bfloat16)], axis=0
    )
    send_tokens = padded_tokens[token_index].reshape(
        data_count, expert_count, capacity, model_width
    )
    send_cotangent = padded_cotangent[token_index].reshape(
        data_count, expert_count, capacity, model_width
    )
    send_gates = padded_gates[slot_table].reshape(data_count, expert_count, capacity)
    arrived = (
        lax.all_to_all(
            lax.all_to_all(send_tokens, "dp", split_axis=0, concat_axis=0, tiled=True),
            "expert",
            split_axis=1,
            concat_axis=1,
            tiled=True,
        ),
        lax.all_to_all(
            lax.all_to_all(send_cotangent, "dp", split_axis=0, concat_axis=0, tiled=True),
            "expert",
            split_axis=1,
            concat_axis=1,
            tiled=True,
        ),
        lax.all_to_all(
            lax.all_to_all(send_gates, "dp", split_axis=0, concat_axis=0, tiled=True),
            "expert",
            split_axis=1,
            concat_axis=1,
            tiled=True,
        ),
    )
    arrived_tokens = arrived[0].reshape(slot_total, model_width)
    routed = expert_grads(
        arrived_tokens,
        arrived[1].reshape(slot_total, model_width),
        arrived[2].reshape(slot_total).astype(jnp.float32),
        expert_weights[0],
    )
    grad_experts = weight_terms(arrived_tokens, routed[2], routed[3], routed[5], routed[4]).astype(
        jnp.bfloat16
    )[None]
    outgoing_input = (
        routed[0].astype(jnp.bfloat16).reshape(data_count, expert_count, capacity, model_width)
    )
    outgoing_gate = routed[1].astype(jnp.bfloat16).reshape(data_count, expert_count, capacity)
    returned = (
        lax.all_to_all(
            lax.all_to_all(outgoing_input, "dp", split_axis=0, concat_axis=0, tiled=True),
            "expert",
            split_axis=1,
            concat_axis=1,
            tiled=True,
        ),
        lax.all_to_all(
            lax.all_to_all(outgoing_gate, "dp", split_axis=0, concat_axis=0, tiled=True),
            "expert",
            split_axis=1,
            concat_axis=1,
            tiled=True,
        ),
    )
    flat_back = returned[0].reshape(slot_total, model_width)
    routed_sum = jnp.sum(flat_back[position].astype(jnp.float32), axis=1)
    grad_gates = returned[1].reshape(slot_total)[position]
    shared = expert_grads(tokens, cotangent, jnp.ones((tok_rows,), jnp.float32), shared_weights)
    grad_tokens = (routed_sum + shared[0]).astype(jnp.bfloat16)
    kept_rows = model_width // data_count
    shared_units = shared_weights.shape[2]
    upstream_cols = shared[5]
    kept = lax.psum_scatter(
        jnp.concatenate(
            [
                contract_rows(tokens, shared[2]),
                contract_rows(tokens, shared[3]),
                contract_rows(upstream_cols, shared[4]),
            ],
            axis=1,
        ),
        "dp",
        scatter_dimension=0,
        tiled=True,
    )
    totals = lax.psum(kept, "expert")
    grad_shared = jnp.transpose(totals.reshape(kept_rows, 3, shared_units), (1, 0, 2))
    return (grad_tokens, grad_gates, grad_experts, grad_shared)


def strict_upper(rows):
    r = lax.broadcasted_iota(jnp.int32, (rows, rows), 0)
    c = lax.broadcasted_iota(jnp.int32, (rows, rows), 1)
    return (r < c).astype(jnp.bfloat16)


def dot32(left, right, dims=((1,), (0,))):
    return lax.dot_general(left, right, (dims, ((), ())), preferred_element_type=jnp.float32)


def route_kernel(group, n, cap, at_ref, gates_ref, *refs):
    pieces, w_refs = refs[:n], refs[n : n + 2]
    parts = refs[n + 2 : 2 * n + 2]
    xs, sy, gg, gu, hb, onehot, yslot, ig = refs[2 * n + 2 :]
    rows, width = gates_ref.shape[3], pieces[0].shape[1]
    gates = jnp.concatenate([gates_ref[s] for s in group], axis=0)
    named = jnp.where(gates > 0, 1.0, 0.0)
    before = dot32(named.reshape(2 * n, rows).astype(jnp.bfloat16), strict_upper(rows))
    before = before.reshape(n, 2, rows)
    slot = lax.broadcasted_iota(jnp.int32, (cap, rows), 0).astype(jnp.float32)
    scales = [[], []]
    for p in range(n):
        for j in range(2):
            hit = (before[p, j][None, :] == slot) & (named[p, j][None, :] > 0)
            hit = jnp.where(hit, 1.0, 0.0)
            onehot[p, j * cap : (j + 1) * cap] = hit.astype(jnp.bfloat16)
            scales[j].append(jnp.sum(hit * gates[p, j][None, :], axis=1, keepdims=True))
        picked_x = dot32(onehot[p], pieces[p][:rows]).astype(jnp.bfloat16)
        picked_y = dot32(onehot[p], pieces[p][rows:])
        for j in range(2):
            here = slice(p * cap, (p + 1) * cap)
            there = slice(j * cap, (j + 1) * cap)
            xs[j, here] = picked_x[there]
            yslot[j, here] = picked_y[there].astype(jnp.bfloat16)
            sy[j, here] = (picked_y[there] * scales[j][p]).astype(jnp.bfloat16)
    hidden_units = w_refs[0].shape[2]
    tile = min(256, hidden_units)
    grads = []
    for j, w in enumerate(w_refs):
        scale = jnp.concatenate(scales[j], axis=0)
        gate_grad = jnp.zeros((n * cap, 1), jnp.float32)
        for f in range(0, hidden_units, tile):
            cols = slice(f, f + tile)
            pre_gate = dot32(xs[j], w[0, :, cols])
            pre_up = dot32(xs[j], w[1, :, cols])
            back = dot32(yslot[j], w[2, :, cols])
            activated, slope = silu_parts(pre_gate)
            hidden = activated * pre_up
            gate_grad += jnp.sum(hidden * back, axis=1, keepdims=True)
            scaled = scale * back
            gg[j, :, cols] = (scaled * pre_up * slope).astype(jnp.bfloat16)
            gu[j, :, cols] = (scaled * activated).astype(jnp.bfloat16)
            hb[j, :, cols] = hidden.astype(jnp.bfloat16)
        ig[j] = (
            dot32(gg[j], w[0], ((1,), (1,))) + dot32(gu[j], w[1], ((1,), (1,)))
        ).astype(jnp.bfloat16)
        grads.append(gate_grad)
    extra = parts[0].shape[0] - rows
    row = lax.broadcasted_iota(jnp.int32, (extra, width), 0)
    block = lax.broadcasted_iota(jnp.int32, (extra, width), 1) // rows
    for p in range(n):
        tail = jnp.zeros((extra, width), jnp.float32)
        for j in range(2):
            here = slice(p * cap, (p + 1) * cap)
            hit = onehot[p, j * cap : (j + 1) * cap].astype(jnp.float32)
            line = jnp.sum(hit * grads[j][here], axis=0, keepdims=True)
            line = jnp.concatenate([line] * (width // rows), axis=1)
            mine = (row == at_ref[2 * j]) & (block == at_ref[2 * j + 1])
            tail = tail + jnp.where(mine, line, 0.0)
        both = jnp.concatenate([ig[j, here] for j in range(2)], axis=0)
        parts[p][:rows] = dot32(onehot[p], both, ((0,), (0,))).astype(parts[p].dtype)
        parts[p][rows:] = tail.astype(jnp.bfloat16).astype(parts[p].dtype)


MIB = 1024 * 1024
IN_SMEM = pl.BlockSpec(memory_space=pltpu.SMEM)
IN_VMEM = pl.BlockSpec(memory_space=pltpu.VMEM)


def route(group, cap, extra, at, gates, pieces, w_own, w_sib):
    n, rows, width = len(pieces), gates.shape[3], pieces[0].shape[1]
    hidden_units = w_own.shape[2]
    slots = n * cap
    shape, scratch = jax.ShapeDtypeStruct, pltpu.VMEM
    bf = jnp.bfloat16
    kinds = [bf if p % 4 else jnp.float32 for p in range(n)]
    out_shape = [shape((rows + extra, width), kind) for kind in kinds]
    out_shape += [shape((2, slots, width), bf)] * 2 + [shape((2, slots, hidden_units), bf)] * 3
    outs = pl.pallas_call(
        functools.partial(route_kernel, group, n, cap),
        out_shape=out_shape,
        in_specs=[IN_SMEM] + [IN_VMEM] * (n + 3),
        out_specs=[IN_VMEM] * (n + 5),
        scratch_shapes=[
            scratch((n, 2 * cap, rows), bf),
            scratch((2, slots, width), bf),
            scratch((2, slots, width), bf),
        ],
        cost_estimate=pl.CostEstimate(
            flops=20 * slots * width * hidden_units,
            bytes_accessed=4 * w_own.size + 16 * slots * width,
            transcendentals=0,
        ),
        compiler_params=pltpu.CompilerParams(vmem_limit_bytes=14 * MIB),
        name="route",
    )(at, gates, *pieces, w_own, w_sib)
    return outs[:n], outs[n:]


def common_kernel(n, first, last, where_ref, *refs):
    pieces, w, refs = refs[:n], refs[n], refs[n + 1 :]
    (own_grad,), refs = (refs[:1], refs[1:]) if first else ((None,), refs)
    (total_in,), refs = ((None,), refs) if first else (refs[:1], refs[1:])
    outs, (x, y, gg, gu, hb) = refs[:-5], refs[-5:]
    rows = pieces[0].shape[0] // 2
    for p in range(n):
        x[p * rows : (p + 1) * rows] = pieces[p][:rows]
        y[p * rows : (p + 1) * rows] = pieces[p][rows:]
    hidden_units = w.shape[2]
    tile = min(256, hidden_units)
    chunk = 4 * rows
    for r in range(0, n * rows, chunk):
        at = slice(r, min(r + chunk, n * rows))
        for f in range(0, hidden_units, tile):
            cols = slice(f, f + tile)
            pre_gate = dot32(x[at], w[0, :, cols])
            pre_up = dot32(x[at], w[1, :, cols])
            back = dot32(y[at], w[2, :, cols])
            activated, slope = silu_parts(pre_gate)
            gg[at, cols] = (back * pre_up * slope).astype(jnp.bfloat16)
            gu[at, cols] = (back * activated).astype(jnp.bfloat16)
            hb[at, cols] = (activated * pre_up).astype(jnp.bfloat16)
    if first:
        own_grad[...] = dot32(gg[:rows], w[0], ((1,), (1,))) + dot32(gu[:rows], w[1], ((1,), (1,)))
    kept = outs[0].shape[1] * (2 if last else 1)
    half = kept // 2
    for i, (left, right) in enumerate(((x, gg), (x, gu), (y, hb))):
        if last:
            core = where_ref[1]
            for out, block in zip(outs, (core, 1 - core)):
                keep = pl.ds(pl.multiple_of(where_ref[0] * kept + block * half, half), half)
                term = dot32(left[:, keep], right[...], ((0,), (0,)))
                term = term + total_in[i, pl.ds(pl.multiple_of(block * half, half), half)]
                out[i] = term.astype(out.dtype)
        else:
            keep = pl.ds(pl.multiple_of(where_ref[0] * kept, kept), kept)
            term = dot32(left[:, keep], right[...], ((0,), (0,)))
            outs[0][i] = term if first else term + total_in[i]


def common(where_at, kept, pieces, w, total, last=False):
    first = total is None
    n, rows, width = len(pieces), pieces[0].shape[0] // 2, pieces[0].shape[1]
    hidden_units = w.shape[2]
    shape, scratch = jax.ShapeDtypeStruct, pltpu.VMEM
    bf, f32 = jnp.bfloat16, jnp.float32
    out_shape = [shape((rows, width), f32)] if first else []
    if last:
        out_shape += [shape((3, kept // 2, hidden_units), dtype) for dtype in (f32, bf)]
    else:
        out_shape += [shape((3, kept, hidden_units), f32)]
    args = list(pieces) + [w] + ([] if first else [total])
    return pl.pallas_call(
        functools.partial(common_kernel, n, first, last),
        out_shape=out_shape,
        in_specs=[IN_SMEM] + [IN_VMEM] * len(args),
        out_specs=[IN_VMEM] * len(out_shape),
        scratch_shapes=[scratch((n * rows, width), bf)] * 2
        + [scratch((n * rows, hidden_units), bf)] * 3,
        cost_estimate=pl.CostEstimate(
            flops=6 * n * rows * hidden_units * (width + kept),
            bytes_accessed=2 * w.size + n * rows * width * 4,
            transcendentals=0,
        ),
        compiler_params=pltpu.CompilerParams(vmem_limit_bytes=14 * MIB),
        name="common",
    )(where_at, *args)


def weights_kernel(groups, *refs):
    saved, (own, sib, xs, sy, gg, gu, hb) = refs[: 5 * groups], refs[5 * groups :]
    for j in (1, 0):
        at = 0
        for g in range(groups):
            slots = saved[5 * g].shape[1]
            for i, into in enumerate((xs, sy, gg, gu, hb)):
                into[at : at + slots] = saved[5 * g + i][j]
            at += slots
        for i, (left, right) in enumerate(((xs, gg), (xs, gu), (sy, hb))):
            out = (own, sib)[j]
            out[i] = dot32(left[...], right[...], ((0,), (0,))).astype(out.dtype)


def weights(saved):
    groups = len(saved)
    flat = [a for group in saved for a in group]
    width, hidden_units = flat[0].shape[2], flat[2].shape[2]
    slots = sum(group[0].shape[1] for group in saved)
    bf, scratch = jnp.bfloat16, pltpu.VMEM
    return pl.pallas_call(
        functools.partial(weights_kernel, groups),
        out_shape=[
            jax.ShapeDtypeStruct((3, width, hidden_units), bf),
            jax.ShapeDtypeStruct((3, width, hidden_units), bf),
        ],
        in_specs=[IN_VMEM] * len(flat),
        out_specs=[IN_VMEM] * 2,
        scratch_shapes=[scratch((slots, width), bf)] * 2 + [scratch((slots, hidden_units), bf)] * 3,
        cost_estimate=pl.CostEstimate(
            flops=12 * slots * width * hidden_units,
            bytes_accessed=slots * (8 * width + 12 * hidden_units),
            transcendentals=0,
        ),
        compiler_params=pltpu.CompilerParams(vmem_limit_bytes=18 * MIB),
        name="weights",
    )(*flat)


def sums_kernel(e_mine, s_mine, e_came, s_came, e_out, s_out, *scratch):
    e_in, s_in, e_res, s_res, sem_in, sem_out = scratch
    count = e_mine.shape[0]
    parts = [(e_mine, e_came, e_in, e_res, e_out, i, i) for i in range(count)]
    parts += [(s_mine, s_came, s_in, s_res, s_out, i, count + i) for i in range(count)]
    bring = [
        pltpu.make_async_copy(came.at[i], into.at[i], sem_in.at[k])
        for _, came, into, _, _, i, k in parts
    ]
    for copy in bring:
        copy.start()
    sends = []
    for (mine, _, into, res, out, i, k), copy in zip(parts, bring):
        copy.wait()
        res[i] = (mine[i].astype(jnp.float32) + into[i].astype(jnp.float32)).astype(res.dtype)
        sends.append(pltpu.make_async_copy(res.at[i], out.at[i], sem_out.at[k]))
        sends[-1].start()
    for copy in sends:
        copy.wait()


def last_sums(e_mine, s_mine, e_came, s_came):
    shape, scratch, dma = jax.ShapeDtypeStruct, pltpu.VMEM, pltpu.SemaphoreType.DMA
    bf, f32 = jnp.bfloat16, jnp.float32
    count = e_mine.shape[0]
    in_place = pl.BlockSpec(memory_space=pl.ANY)
    return pl.pallas_call(
        sums_kernel,
        out_shape=[shape(e_mine.shape, bf), shape(s_mine.shape, f32)],
        in_specs=[IN_VMEM] * 2 + [in_place] * 2,
        out_specs=[in_place] * 2,
        scratch_shapes=[scratch(e_came.shape, bf), scratch(s_came.shape, bf)]
        + [scratch(e_mine.shape, bf), scratch(s_mine.shape, f32)]
        + [dma((2 * count,)), dma((2 * count,))],
        compiler_params=pltpu.CompilerParams(vmem_limit_bytes=16 * MIB),
        name="sums",
    )(e_mine, s_mine, e_came, s_came)


def hold_kernel(array, out, sem):
    copy = pltpu.make_async_copy(array, out, sem.at[0])
    copy.start()
    copy.wait()


def hold(array):
    return pl.pallas_call(
        hold_kernel,
        out_shape=jax.ShapeDtypeStruct(array.shape, array.dtype),
        in_specs=[pl.BlockSpec(memory_space=pltpu.HBM)],
        out_specs=IN_VMEM,
        scratch_shapes=[pltpu.SemaphoreType.DMA((1,))],
        compiler_params=pltpu.CompilerParams(vmem_limit_bytes=4 * MIB),
        name="hold",
    )(array)


def join_kernel(left, right, out, sem):
    rows = left.shape[0]
    copies = [
        pltpu.make_async_copy(left, out.at[pl.ds(0, rows)], sem.at[0]),
        pltpu.make_async_copy(right, out.at[pl.ds(rows, rows)], sem.at[1]),
    ]
    for copy in copies:
        copy.start()
    for copy in copies:
        copy.wait()


def join(left, right):
    rows, width = left.shape
    return pl.pallas_call(
        join_kernel,
        out_shape=jax.ShapeDtypeStruct((2 * rows, width), left.dtype),
        in_specs=[pl.BlockSpec(memory_space=pltpu.HBM)] * 2,
        out_specs=IN_VMEM,
        scratch_shapes=[pltpu.SemaphoreType.DMA((2,))],
        compiler_params=pltpu.CompilerParams(vmem_limit_bytes=60 * MIB),
        name="join",
    )(left, right)


def finish_kernel(terms, ids_ref, *refs):
    sums, own_grad, (tokens_out, gates_out) = refs[:terms], refs[terms], refs[terms + 1 :]
    top_count, rows = ids_ref.shape
    total = sums[0][...].astype(jnp.float32)
    for ref in sums[1:]:
        total = total + ref[...].astype(jnp.float32)
    tokens_out[...] = (total[:rows] + own_grad[...]).astype(tokens_out.dtype)
    blocks = total.shape[1] // rows
    by_expert = jnp.concatenate(
        [
            total[r : r + 1, b * rows : (b + 1) * rows]
            for r in range(rows, total.shape[0])
            for b in range(blocks)
        ],
        axis=0,
    )
    expert = lax.broadcasted_iota(jnp.int32, by_expert.shape, 0)
    picked = [
        jnp.sum(jnp.where(ids_ref[k : k + 1] == expert, by_expert, 0.0), axis=0, keepdims=True)
        for k in range(top_count)
    ]
    gates_out[...] = jnp.concatenate(picked, axis=0).astype(gates_out.dtype)


def finish(expert_ids, sums, own_grad):
    rows, top_count = expert_ids.shape
    tokens, gates = pl.pallas_call(
        functools.partial(finish_kernel, len(sums)),
        out_shape=[
            jax.ShapeDtypeStruct(own_grad.shape, jnp.bfloat16),
            jax.ShapeDtypeStruct((top_count, rows), jnp.bfloat16),
        ],
        in_specs=[IN_VMEM] * (len(sums) + 2),
        out_specs=[IN_VMEM] * 2,
        compiler_params=pltpu.CompilerParams(vmem_limit_bytes=8 * MIB),
        name="finish",
    )(expert_ids.T, *sums, own_grad)
    return tokens, gates.T


def shared_rows(tokens, cotangent, expert_ids, gate_weights, expert_weights, shared_weights):
    return shared_rows_body(
        tokens, cotangent, expert_ids, gate_weights, expert_weights, shared_weights
    )


def shared_rows_body(tokens, cotangent, expert_ids, gate_weights, expert_weights, shared_weights):
    rows, width = tokens.shape
    top_count = expert_ids.shape[1]
    data_count, expert_count = lax.axis_size("dp"), lax.axis_size("expert")
    devices = data_count * expert_count
    cap = capacity_of(rows, top_count, devices)
    planes = expert_count // 2
    bf, f32 = jnp.bfloat16, jnp.float32
    me_dp, me_ex = lax.axis_index("dp"), lax.axis_index("expert")
    routes = {
        "x": ("expert", [(e, e ^ 1) for e in range(expert_count)]),
        "+": ("expert", [(e, (e + 2) % expert_count) for e in range(expert_count)]),
        "-": ("expert", [(e, (e - 2) % expert_count) for e in range(expert_count)]),
        "y": ("dp", [(d, d ^ 2) for d in range(data_count)]),
        "core": ("dp", [(d, d ^ 1) for d in range(data_count)]),
    }

    def send(way, array):
        return lax.ppermute(array, *routes[way])

    w_own = expert_weights[0]
    own = join(tokens, cotangent)
    w_sib = send("core", w_own)
    w_sib = hold(w_sib)

    c, x, y, d = [own] + [None] * 3, [None] * 4, [None] * 4, [None] * 4
    c[1] = send("+", c[0])
    c[2] = send("+", c[1])
    c[3] = send("-", c[0])
    for s in range(planes):
        x[s] = send("x", c[s])
        y[s] = send("y", c[s])
    d[0] = send("x", y[0])
    d[1] = send("+", d[0])
    d[2] = send("y", x[2])
    d[3] = send("x", y[3])

    matches = expert_ids[:, :, None] == jnp.arange(devices, dtype=jnp.int32)
    by_expert = jnp.sum(jnp.where(matches, gate_weights[:, :, None].astype(f32), 0.0), axis=1)
    by_expert = by_expert.T.astype(bf).reshape(data_count // 2, 2, expert_count, rows)
    outward = jnp.stack([by_expert, by_expert[:, ::-1]], axis=3).reshape(devices, 2, rows)
    inward = lax.all_to_all(outward, ("dp", "expert"), 0, 0, tiled=True)
    order = []
    for s in range(planes):
        plane = (me_ex // 2 + planes - s) % planes
        for dy, dx in ((0, 0), (0, 1), (1, 0), (1, 1)):
            source = (me_dp ^ (2 * dy)) * expert_count + plane * 2 + (me_ex % 2 ^ dx)
            order.append(source)
    pick = jnp.stack(order)[:, None] == jnp.arange(devices, dtype=jnp.int32)[None, :]
    pick = pick.astype(bf)
    gates = jnp.dot(pick, inward.reshape(devices, 2 * rows), preferred_element_type=f32)
    gates = gates.reshape(planes, 4, 2, rows)

    extra = 8 * (-(-devices * rows // (8 * width)))
    blocks = width // rows
    me = me_dp * expert_count + me_ex
    sibling = (me_dp ^ 1) * expert_count + me_ex
    at = jnp.stack([me // blocks, me % blocks, sibling // blocks, sibling % blocks])
    at = at.astype(jnp.int32)
    part, saved = [None] * 4, []
    for group in ((0,), (1,), (2,), (3,)):
        pieces = [piece for s in group for piece in (c[s], x[s], y[s], d[s])]
        sums, keep = route(group, cap, extra, at, gates, pieces, w_own, w_sib)
        saved.append(keep)
        for i, s in enumerate(group):
            part[s] = sums[4 * i : 4 * i + 4]
    pc, px, py, pd = zip(*part)

    where_at = jnp.stack([me_dp // 2, me_dp % 2]).astype(jnp.int32)
    kept = 2 * (width // data_count)
    pieces = (c[0], x[0], y[0], c[1])
    shared_grad, total = common(where_at, kept, pieces, shared_weights, None)
    pieces = (d[0], y[1], x[1], c[2])
    (total,) = common(where_at, kept, pieces, shared_weights, total)
    pieces = (c[3], x[2], y[2])
    (total,) = common(where_at, kept, pieces, shared_weights, total)
    pieces = (d[1], x[3], y[3], d[2], d[3])
    mine, other = common(where_at, kept, pieces, shared_weights, total, last=True)

    def plus(*terms):
        total = terms[0].astype(f32)
        for term in terms[1:]:
            total = total + term.astype(f32)
        return total

    def home_x(array):
        return send("x", array.astype(bf))

    def home_y(array):
        return send("y", array.astype(bf))

    part_x, part_y = list(px), list(py)
    for s in range(planes):
        if s % 2:
            part_y[s] = plus(py[s], send("x", pd[s]))
        else:
            part_x[s] = plus(px[s], send("y", pd[s]))
    arrived = [(pc[s], home_x(part_x[s]), home_y(part_y[s])) for s in range(planes)]
    c3 = arrived[3] + (send("+", plus(*arrived[2]).astype(bf)),)
    sums = arrived[0] + (send("-", plus(*arrived[1]).astype(bf)),)
    sums += (send("+", plus(*c3).astype(bf)),)
    grad_tokens, grad_gates = finish(expert_ids, sums, shared_grad)

    mine_experts, for_sib = weights(saved)
    came = send("core", for_sib)
    came_shared = send("core", other)
    grad_experts, grad_shared = last_sums(mine_experts, mine, came, came_shared)
    grad_experts = grad_experts[None]
    return (grad_tokens, grad_gates, grad_experts, grad_shared)


def solution(mesh):
    placed = (
        P(("dp", "expert"), None),
        P(("dp", "expert"), None),
        P(("dp", "expert"), None),
        P(("dp", "expert"), None),
        P(("dp", "expert"), None, None, None),
        P(),
    )
    share = mesh.shape["dp"] == 4 and mesh.shape["expert"] == 8
    return jax.shard_map(
        shared_rows if share else shards,
        mesh=mesh,
        in_specs=placed,
        out_specs=(
            P(("dp", "expert"), None),
            P(("dp", "expert"), None),
            P(("dp", "expert"), None, None, None),
            P(None, "dp", None),
        ),
        check_vma=False,
    )
```
